128 devices in a mesh: table: 16 (over z, y_lo, core), dp: 8 (over x, y_hi).
Axes of the slice: x: 4, y: 4 (y_hi: 2, y_lo: 2; y = y_hi * 2 + y_lo), z: 4, core: 2. Of those that a mesh axis runs over, the one named last changes fastest.
Arguments:
- own_table: bfloat16 [20480, 128], P('table'), may hold values from -6 to 6
- own_accum: float32 [20480], P('table'), may hold values from 0.5 to 8
- sectioned_rows: bfloat16 [16, 768, 128], P(None, 'dp'), may hold values from -6 to 6
- sectioned_accum: float32 [16, 768], replicated, may hold values from 0.5 to 8
- fold_pairs: int32 [16], replicated, may hold values from 0 to 15, each once
- slab_ids: int32 [16, 6], replicated, may hold values from 0 to 5, each once within a row
- bag_blocks: int32 [32768, 16, 4], P('dp', 'table'), may hold values from 0 to 15, as said below
- bag_counts: int32 [32768, 16], P('dp', 'table'), may hold values from 1 to 4
- bag_weights: bfloat16 [32768, 16, 4, 128], P('dp', 'table'), may hold values from -0.25 to 0.25
- top_weight: bfloat16 [2048, 1024], replicated, may hold values from -0.125 to 0.125
- hidden_grad: bfloat16 [32768, 1024], P(('dp', 'table')), may hold values from -6 to 6
Outputs:
- new_table: bfloat16 [32768, 128], P('table')
- new_accum: float32 [32768], P(('table', 'dp'))
- hidden: bfloat16 [32768, 1024], P(('dp', 'table'))
The draws below stay inside these ranges and needn't reach their ends.
Inputs may be any that keep to these rules, and one draw needn't show every extreme that they name: `bag_blocks`: the used slots (k < bag_counts) of one bag in one feature name distinct blocks; block 15 and block 0 are both read by some bag in every draw. Slots k >= bag_counts[b, t] are unused. `fold_pairs`: A permutation. `slab_ids`: each row a permutation.
All inputs are finite; a program needn't handle non-finite values.
Results may differ from the reference program's by a relative error of at most 0.0065.
Values may be sent and summed in bfloat16 or wider, within the bound.
No kernel may reach another device: no remote copies, remote signals or barrier semaphores. Data moves between devices by JAX's collectives and lax.ppermute only.
A program may use at most 128 MiB of HBM per device.

```python
import math
import jax
import jax.numpy as jnp
from jax import lax

E = 128
H = 1024
BLK = 128
R = 10
SLAB = 6
K = 4
BAG_DEV = 4096
FEATURES = 16
BAGS = 32768


def draw_bag_blocks(key, part):
    heat_key, noise_key = jax.random.split(jax.random.fold_in(key, 41))
    block_count = R + SLAB
    heat = jax.random.randint(heat_key, (FEATURES, block_count), 0, 2048)
    noise = jax.random.randint(noise_key, (BAGS, FEATURES, block_count), 0, 4096)
    column = jnp.arange(block_count, dtype=jnp.int32)
    bag_index = jnp.arange(BAGS, dtype=jnp.int32)[:, None, None]
    forced = (bag_index == 0) & (column == block_count - 1) | (bag_index == 1) & (column == 0)
    scores = (heat[None] + noise + forced.astype(jnp.int32) * 65536) * 64 + column
    return lax.top_k(scores, K)[1].astype(jnp.int32)


def place_ends(result, stream_key, low, largest):
    index_at = [jax.random.randint(jax.random.fold_in(stream_key, axis), (), 0, length) for axis, length in enumerate(result.shape)]
    longest = result.shape.index(max(result.shape))
    beside = index_at[:longest] + [(index_at[longest] + 1) % result.shape[longest]] + index_at[longest + 1:]
    return result.at[tuple(index_at)].set(low).at[tuple(beside)].set(largest)


def block_scale(stream_key, shape, pieces, smallest, high):
    factor_of = 1.0
    for position, blocks in pieces:
        steps = jax.random.uniform(jax.random.fold_in(jax.random.fold_in(stream_key, 6), position), (blocks,), jnp.float32, smallest / len(pieces), high / len(pieces))
        factor_of = factor_of * jnp.repeat(jnp.exp(steps), shape[position] // blocks).reshape((-1,) + (1,) * (len(shape) - 1 - position))
    return factor_of


def bell_draw(stream_key, extent, spread, limit, cuts=(), held_as=jnp.bfloat16):
    entries = spread * jax.random.normal(stream_key, extent, jnp.float32)
    if cuts:
        entries = entries * block_scale(stream_key, extent, cuts, -0.22, 0.18)
    return jnp.clip(entries, -limit, limit).astype(held_as)


def setup_inputs(seed: int = 0) -> dict:
    splits = jax.random.split(jax.random.key(seed), 12)
    own_table = bell_draw(splits[0], (FEATURES * R * BLK, E), 1.0, 6.0, ((0, 16),))
    own_accum = jnp.clip(jnp.exp(math.log(8.0) - 2.7725887 * jax.random.uniform(splits[1], (FEATURES * R * BLK,), jnp.float32) ** block_scale(splits[1], (FEATURES * R * BLK,), ((0, 16),), -0.2, 0.2)), 0.5, 8.0)
    sectioned_rows = bell_draw(splits[2], (FEATURES, SLAB * BLK, E), 1.0, 6.0, ((1, 8),))
    sectioned_accum = jnp.clip(jnp.exp(jax.random.uniform(splits[3], (FEATURES, SLAB * BLK), jnp.float32, math.log(0.5), math.log(8.0))), 0.5, 8.0)
    fold_pairs = jax.random.permutation(splits[4], FEATURES).astype(jnp.int32)
    slab_ids = jax.vmap(lambda own: jax.random.permutation(own, SLAB))(jax.random.split(splits[5], FEATURES)).reshape((FEATURES, SLAB)).astype(jnp.int32)
    bag_blocks = draw_bag_blocks(jax.random.fold_in(splits[11], 71), 0)
    bag_counts = place_ends(jax.random.randint(splits[7], (BAGS, FEATURES), 1, K + 1), jax.random.fold_in(splits[7], 1), 1, K).astype(jnp.int32)
    bag_weights = bell_draw(splits[8], (BAGS, FEATURES, K, BLK), (K * BLK) ** -0.5, 0.25, ((0, 8), (1, 16)))
    top_weight = bell_draw(splits[9], (FEATURES * E, H), (FEATURES * E) ** -0.5, 0.125)
    hidden_grad = bell_draw(splits[10], (BAGS, H), 1.0, 6.0, ((0, 128),))
    return dict(own_table=own_table, own_accum=own_accum, sectioned_rows=sectioned_rows, sectioned_accum=sectioned_accum, fold_pairs=fold_pairs, slab_ids=slab_ids, bag_blocks=bag_blocks, bag_counts=bag_counts, bag_weights=bag_weights, top_weight=top_weight, hidden_grad=hidden_grad)


learn_rate = 0.5
ada_epsilon = 1e-08

def gate_slope(preact):
    sigmoid_part = jax.nn.sigmoid(preact)
    return sigmoid_part * (1.0 + preact * (1.0 - sigmoid_part))

def reference(own_table, own_accum, sectioned_rows, sectioned_accum, fold_pairs, slab_ids, bag_blocks, bag_counts, bag_weights, top_weight, hidden_grad):
    block_count = R + SLAB
    block_order = slab_ids[fold_pairs]
    sectioned = sectioned_rows[fold_pairs].reshape(FEATURES, SLAB, BLK, E)
    folded = jnp.take_along_axis(sectioned, block_order[:, :, None, None], axis=1).reshape(FEATURES, SLAB * BLK, E)
    table_rows = jnp.concatenate([own_table.reshape(FEATURES, R * BLK, E), folded], axis=1)
    sectioned_state = sectioned_accum[fold_pairs].reshape(FEATURES, SLAB, BLK)
    folded_state = jnp.take_along_axis(sectioned_state, block_order[:, :, None], axis=1).reshape(FEATURES, SLAB * BLK)
    merged_accum = jnp.concatenate([own_accum.reshape(FEATURES, R * BLK), folded_state], axis=1)
    column = jnp.arange(block_count, dtype=jnp.int32)
    slot_index = jnp.arange(K, dtype=jnp.int32)
    group_count = BAGS // BAG_DEV

    def bag_matrix(feature, group):
        start = (group * BAG_DEV).astype(jnp.int32)
        blocks = lax.dynamic_slice_in_dim(lax.dynamic_index_in_dim(bag_blocks, feature, 1, keepdims=False), start, BAG_DEV, 0)
        counts = lax.dynamic_slice_in_dim(lax.dynamic_index_in_dim(bag_counts, feature, 1, keepdims=False), start, BAG_DEV, 0)
        weights = lax.dynamic_slice_in_dim(lax.dynamic_index_in_dim(bag_weights, feature, 1, keepdims=False), start, BAG_DEV, 0)
        slot_hit = (blocks[:, :, None] == column) & (slot_index[None, :, None] < counts[:, None, None])
        matrix = jnp.einsum('nkm,nkr->nmr', slot_hit.astype(jnp.float32), weights.astype(jnp.float32))
        return matrix.astype(jnp.bfloat16).reshape(BAG_DEV, block_count * BLK)

    def pool_feature(feature):
        rows = lax.dynamic_index_in_dim(table_rows, feature, 0, keepdims=False)

        def pool_group(group):
            return jnp.dot(bag_matrix(feature, group), rows, preferred_element_type=jnp.float32).astype(jnp.bfloat16)
        return lax.map(pool_group, jnp.arange(group_count, dtype=jnp.int32)).reshape(BAGS, E)
    pooled = lax.map(pool_feature, jnp.arange(FEATURES, dtype=jnp.int32))
    concat_rows = jnp.transpose(pooled, (1, 0, 2)).reshape(BAGS, FEATURES * E)
    preact = jnp.dot(concat_rows, top_weight, preferred_element_type=jnp.float32)
    hidden = jax.nn.silu(preact).astype(jnp.bfloat16)
    pre_grad = (hidden_grad.astype(jnp.float32) * gate_slope(preact)).astype(jnp.bfloat16)
    concat_grad = jnp.dot(pre_grad, top_weight.T, preferred_element_type=jnp.float32).astype(jnp.bfloat16)
    pooled_grad = jnp.transpose(concat_grad.reshape(BAGS, FEATURES, E), (1, 0, 2))

    def grad_feature(feature):
        grads_here = lax.dynamic_index_in_dim(pooled_grad, feature, 0, keepdims=False)

        def add_group(total, group):
            part = lax.dynamic_slice_in_dim(grads_here, (group * BAG_DEV).astype(jnp.int32), BAG_DEV, 0)
            return (total + jnp.dot(bag_matrix(feature, group).T, part, preferred_element_type=jnp.float32), None)
        total, unused = lax.scan(add_group, jnp.zeros((block_count * BLK, E), jnp.float32), jnp.arange(group_count, dtype=jnp.int32))
        return total
    row_grad = lax.map(grad_feature, jnp.arange(FEATURES, dtype=jnp.int32))
    new_accum = merged_accum + lax.optimization_barrier(jnp.mean(row_grad * row_grad, axis=2))
    step_size = learn_rate / (jnp.sqrt(new_accum) + ada_epsilon)
    new_table = (table_rows.astype(jnp.float32) - step_size[:, :, None] * row_grad).astype(jnp.bfloat16)
    return (new_table.reshape(FEATURES * block_count * BLK, E), new_accum.reshape(FEATURES * block_count * BLK), hidden)
```

```python
import functools

import jax
import jax.numpy as jnp
from jax import lax
from jax.experimental import pallas as pl
from jax.experimental.pallas import tpu as pltpu
from jax.sharding import PartitionSpec as P

E = 128
BLK = 128
R = 10
SLAB = 6
K = 4
NB = R + SLAB

learn_rate = 0.5
ada_epsilon = 1e-08


def build_body(rows, sub, blk_ref, cnt_ref, w_ref, m_ref, eff_ref):
    base = pl.multiple_of(pl.program_id(0) * rows, rows)
    blk = blk_ref[:, pl.ds(base, rows)]
    cnt = cnt_ref[:, pl.ds(base, rows)]
    slot = lax.broadcasted_iota(jnp.int32, (K, rows), 0)
    used = jnp.where(slot < cnt, blk, NB).astype(jnp.float32)
    used = jnp.concatenate([used, jnp.full((8 - K, rows), float(NB), jnp.float32)], axis=0)
    eff_ref[...] = used.T

    def group(g, carry):
        at = pl.multiple_of(g * sub, sub)
        cols = eff_ref[pl.ds(at, sub), :]
        names = [jnp.broadcast_to(cols[:, k:k + 1], (sub, BLK)).astype(jnp.bfloat16) for k in range(K)]
        parts = [w_ref[k, pl.ds(at, sub), :] for k in range(K)]
        zero = jnp.zeros((sub, BLK), jnp.bfloat16)
        for m in range(NB):
            acc = zero
            for k in range(K):
                acc = jnp.where(names[k] == jnp.bfloat16(m), parts[k], acc)
            m_ref[pl.ds(at, sub), m * BLK:(m + 1) * BLK] = acc
        return carry
    lax.fori_loop(0, rows // sub, group, 0)

def build(blocks, counts, weights, rows=512, sub=64):
    bags = blocks.shape[1]
    return pl.pallas_call(
        functools.partial(build_body, rows, sub),
        grid=(bags // rows,),
        in_specs=[pl.BlockSpec((K, bags), lambda i: (0, 0)),
                  pl.BlockSpec((1, bags), lambda i: (0, 0)),
                  pl.BlockSpec((K, rows, BLK), lambda i: (0, i, 0))],
        out_specs=pl.BlockSpec((rows, NB * BLK), lambda i: (i, 0)),
        out_shape=jax.ShapeDtypeStruct((bags, NB * BLK), jnp.bfloat16),
        scratch_shapes=[pltpu.VMEM((rows, 8), jnp.float32)],
        cost_estimate=pl.CostEstimate(flops=bags*NB*BLK*8, bytes_accessed=bags*(NB+K)*BLK*2, transcendentals=0),
        name="build",
    )(blocks, counts, weights)

def pool_body(order_ref, m_ref, own_ref, slab_ref, out_ref, table_ref):
    @pl.when(pl.program_id(0) == 0)
    def _():
        table_ref[0:R * BLK, :] = own_ref[...]
        for j in range(SLAB):
            at = pl.multiple_of(order_ref[j] * BLK, BLK)
            table_ref[(R + j) * BLK:(R + j + 1) * BLK, :] = slab_ref[pl.ds(at, BLK), :]
    out_ref[...] = jnp.dot(m_ref[...], table_ref[...], preferred_element_type=jnp.float32).astype(jnp.bfloat16)

def pool(order, matrix, own, slab, rows=1024):
    bags = matrix.shape[0]
    return pl.pallas_call(
        pool_body,
        grid_spec=pltpu.PrefetchScalarGridSpec(
            num_scalar_prefetch=1, grid=(bags // rows,),
            in_specs=[pl.BlockSpec((rows, NB * BLK), lambda i, o: (i, 0)),
                      pl.BlockSpec((R * BLK, E), lambda i, o: (0, 0)),
                      pl.BlockSpec((SLAB * BLK, E), lambda i, o: (0, 0))],
            out_specs=[pl.BlockSpec((rows, E), lambda i, o: (i, 0)),
                       pl.BlockSpec((NB * BLK, E), lambda i, o: (0, 0))]),
        out_shape=[jax.ShapeDtypeStruct((bags, E), jnp.bfloat16),
                   jax.ShapeDtypeStruct((NB * BLK, E), jnp.bfloat16)],
        cost_estimate=pl.CostEstimate(flops=2*bags*NB*BLK*E, bytes_accessed=bags*NB*BLK*2, transcendentals=0),
        name="pool",
    )(order, matrix, own, slab)

def grad_body(m_ref, g_ref, out_ref, acc_ref):
    step = pl.program_id(0)
    part = jnp.dot(g_ref[...].T, m_ref[...], preferred_element_type=jnp.float32)
    @pl.when(step == 0)
    def _():
        acc_ref[...] = part
    @pl.when(step > 0)
    def _():
        acc_ref[...] += part
    @pl.when(step == pl.num_programs(0) - 1)
    def _():
        for m in range(NB):
            out_ref[m * BLK:(m + 1) * BLK, :] = acc_ref[:, m * BLK:(m + 1) * BLK].T.astype(jnp.bfloat16)

def grad(matrix, g, rows=512):
    bags = matrix.shape[0]
    return pl.pallas_call(
        grad_body,
        grid=(bags // rows,),
        in_specs=[pl.BlockSpec((rows, NB * BLK), lambda i: (i, 0)),
                  pl.BlockSpec((rows, E), lambda i: (i, 0))],
        out_specs=pl.BlockSpec((NB * BLK, E), lambda i: (0, 0)),
        out_shape=jax.ShapeDtypeStruct((NB * BLK, E), jnp.bfloat16),
        scratch_shapes=[pltpu.VMEM((E, NB * BLK), jnp.float32)],
        cost_estimate=pl.CostEstimate(flops=2*bags*NB*BLK*E, bytes_accessed=bags*NB*BLK*2, transcendentals=0),
        name="grad",
    )(matrix, g)

def mlp_body(fan, pair, g_ref, tw_hbm, hg_ref, hid_ref, cg_ref, tw_ref, acc_ref, pre_ref, sem):
    wide = pair * E
    steps = fan // pair
    for p in range(steps):
        pltpu.make_async_copy(tw_hbm.at[pl.ds(p * wide, wide), :], tw_ref.at[pl.ds(p * wide, wide), :], sem.at[p]).start()
    for p in range(steps):
        pltpu.make_async_copy(tw_hbm.at[pl.ds(p * wide, wide), :], tw_ref.at[pl.ds(p * wide, wide), :], sem.at[p]).wait()
        left = jnp.concatenate([g_ref[p * pair + q] for q in range(pair)], axis=1)
        part = jnp.dot(left, tw_ref[p * wide:(p + 1) * wide, :], preferred_element_type=jnp.float32)
        if p == 0:
            acc_ref[...] = part
        else:
            acc_ref[...] += part
    pre = acc_ref[...]
    s = jax.nn.sigmoid(pre)
    hid_ref[...] = (pre * s).astype(jnp.bfloat16)
    slope = s * (1.0 + pre * (1.0 - s))
    pre_ref[...] = (hg_ref[...].astype(jnp.float32) * slope).astype(jnp.bfloat16)
    for p in range(steps):
        out = lax.dot_general(pre_ref[...], tw_ref[p * wide:(p + 1) * wide, :], (((1,), (1,)), ((), ())),
                              preferred_element_type=jnp.float32).astype(jnp.bfloat16)
        for q in range(pair):
            cg_ref[p * pair + q] = out[:, q * E:(q + 1) * E]

def mlp(g, tw, hg, pair=2):
    fan, rows, _ = g.shape
    H = tw.shape[1]
    vm = pl.BlockSpec(memory_space=pltpu.VMEM)
    return pl.pallas_call(
        functools.partial(mlp_body, fan, pair),
        in_specs=[vm, pl.BlockSpec(memory_space=pl.ANY), vm],
        out_specs=[vm, vm],
        out_shape=[jax.ShapeDtypeStruct((rows, H), jnp.bfloat16),
                   jax.ShapeDtypeStruct((fan, rows, E), jnp.bfloat16)],
        scratch_shapes=[pltpu.VMEM(tw.shape, jnp.bfloat16), pltpu.VMEM((rows, H), jnp.float32),
                        pltpu.VMEM((rows, H), jnp.bfloat16), pltpu.SemaphoreType.DMA((fan // pair,))],
        cost_estimate=pl.CostEstimate(flops=4*rows*tw.size, bytes_accessed=tw.size*2, transcendentals=rows*H),
        name="mlp",
    )(g, tw, hg)


def everyone(block, axis):
    fan = lax.axis_size(axis)
    copies = jnp.broadcast_to(block[None], (fan,) + block.shape)
    return lax.all_to_all(copies, axis, split_axis=0, concat_axis=0, tiled=True)


def shards(
    own_table,
    own_accum,
    sectioned_rows,
    sectioned_accum,
    fold_pairs,
    slab_ids,
    bag_blocks,
    bag_counts,
    bag_weights,
    top_weight,
    hidden_grad,
):
    tables = lax.axis_size("table")
    parts = lax.axis_size("dp")
    partner = fold_pairs[lax.axis_index("table")]
    block_order = slab_ids[partner]
    piece = lax.dynamic_index_in_dim(sectioned_rows, partner, 0, keepdims=False)
    slab_rows = everyone(piece, "dp").reshape(SLAB * BLK, E)
    bag_total = bag_blocks.shape[0]
    local_bags = bag_total // tables
    matrix = build(
        bag_blocks[:, 0, :].T,
        bag_counts.reshape(1, bag_total),
        jnp.transpose(bag_weights[:, 0], (1, 0, 2)),
    )
    pooled, table_rows = pool(block_order, matrix, own_table, slab_rows)
    gathered = lax.all_to_all(
        pooled.reshape(tables, local_bags, E), "table", split_axis=0, concat_axis=0, tiled=True
    )
    hidden, concat_grad = mlp(gathered, top_weight, hidden_grad)
    returned = lax.all_to_all(concat_grad, "table", split_axis=0, concat_axis=0, tiled=True)
    row_grad = grad(matrix, returned.reshape(bag_total, E))

    share = NB * BLK // parts
    start = lax.axis_index("dp") * share
    state = lax.dynamic_index_in_dim(sectioned_accum, partner, 0, keepdims=False)
    folded_state = jnp.take(state.reshape(SLAB, BLK), block_order, axis=0).reshape(SLAB * BLK)
    merged_accum = jnp.concatenate([own_accum, folded_state], axis=0)
    accum = lax.dynamic_slice_in_dim(merged_accum, start, share, 0)
    rows = lax.dynamic_slice_in_dim(table_rows, start, share, 0)
    received = lax.all_to_all(
        row_grad.reshape(parts, share, E), "dp", split_axis=0, concat_axis=0, tiled=True
    )
    total = jnp.sum(received.astype(jnp.float32), axis=0)
    new_accum = accum + jnp.mean(total * total, axis=1)
    step_size = learn_rate / (jnp.sqrt(new_accum) + ada_epsilon)
    new_rows = (rows.astype(jnp.float32) - step_size[:, None] * total).astype(jnp.bfloat16)
    new_table = everyone(new_rows, "dp").reshape(NB * BLK, E)
    return (new_table, new_accum, hidden)


def solution(mesh):
    placed = (
        P("table", None),
        P("table"),
        P(None, "dp", None),
        P(),
        P(),
        P(),
        P("dp", "table", None),
        P("dp", "table"),
        P("dp", "table", None, None),
        P(),
        P(("dp", "table"), None),
    )
    return jax.shard_map(
        shards,
        mesh=mesh,
        in_specs=placed,
        out_specs=(P("table", None), P(("table", "dp")), P(("dp", "table"), None)),
        check_vma=False,
    )
```

```python
import functools

import jax
import jax.numpy as jnp
from jax import lax
from jax.experimental import pallas as pl
from jax.experimental.pallas import tpu as pltpu
from jax.sharding import PartitionSpec as P

E = 128
BLK = 128
R = 10
SLAB = 6
K = 4
NB = R + SLAB
TILE = 16

learn_rate = 0.5
ada_epsilon = 1e-08

ANY = pl.BlockSpec(memory_space=pl.ANY)
SMEM = pl.BlockSpec(memory_space=pltpu.SMEM)
VMEM = pl.BlockSpec(memory_space=pltpu.VMEM)


def spread_body(half, block_ref, count_ref, weight_ref, out_ref, perm_ref, part_ref):
    step = pl.program_id(0)
    groups = out_ref.shape[0]
    wide = K * BLK

    @pl.when(step == 0)
    def _():
        row = lax.broadcasted_iota(jnp.int32, (wide, BLK), 0)
        lane = lax.broadcasted_iota(jnp.int32, (wide, BLK), 1)
        for k in range(K):
            perm_ref[k] = jnp.where(row == lane * K + k, 1.0, 0.0).astype(jnp.bfloat16)

    for g in range(groups):
        turned = jnp.concatenate([weight_ref[g, BLK * n : BLK * (n + 1), :].T for n in range(K)], axis=1)
        for k in range(0, K, 2):
            right = jnp.concatenate([perm_ref[k], perm_ref[k + 1]], axis=1)
            got = jnp.dot(turned, right, preferred_element_type=jnp.float32).astype(jnp.bfloat16)
            part_ref[g, k] = got[:, :BLK]
            part_ref[g, k + 1] = got[:, BLK:]

    for g in range(groups):
        base = pl.multiple_of(((step * groups + g) * 2 + half) * BLK, BLK)
        blocks = block_ref[:, pl.ds(base, BLK)]
        counts = count_ref[:, pl.ds(base, BLK)]
        names = []
        for k in range(K):
            name = jnp.where(counts > k, blocks[k : k + 1, :], NB).astype(jnp.float32)
            names.append(jnp.broadcast_to(name, (TILE, BLK)).astype(jnp.bfloat16))
        for m in range(NB):
            hits = [names[k] == jnp.bfloat16(m) for k in range(K)]
            for s in range(0, BLK, TILE):
                value = jnp.zeros((TILE, BLK), jnp.bfloat16)
                for k in range(K):
                    value = jnp.where(hits[k], part_ref[g, k, s : s + TILE, :], value)
                out_ref[g, m * BLK + s : m * BLK + s + TILE, :] = value


def spread(blocks, counts, weights, half, join=2):
    bags = blocks.shape[1]
    groups = bags // (2 * BLK)
    return pl.pallas_call(
        functools.partial(spread_body, half),
        grid=(groups // join,),
        in_specs=[
            pl.BlockSpec((K, bags), lambda i: (0, 0)),
            pl.BlockSpec((1, bags), lambda i: (0, 0)),
            pl.BlockSpec((join, None, K * BLK, BLK), lambda i: (i, half, 0, 0)),
        ],
        out_specs=pl.BlockSpec((join, NB * BLK, BLK), lambda i: (i, 0, 0)),
        out_shape=jax.ShapeDtypeStruct((groups, NB * BLK, BLK), jnp.bfloat16),
        scratch_shapes=[
            pltpu.VMEM((K, K * BLK, BLK), jnp.bfloat16),
            pltpu.VMEM((join, K, BLK, BLK), jnp.bfloat16),
        ],
        cost_estimate=pl.CostEstimate(
            flops=bags * NB * BLK * 64, bytes_accessed=bags * (NB + K) * BLK, transcendentals=0
        ),
        name="spread",
    )(blocks, counts, weights.reshape(groups, 2, K * BLK, BLK))


def merge(order_ref, own_ref, slab_ref, table_ref, turned_ref):
    table_ref[0 : R * BLK, :] = own_ref[...]
    for j in range(SLAB):
        at = pl.multiple_of(order_ref[j] * BLK, BLK)
        table_ref[(R + j) * BLK : (R + j + 1) * BLK, :] = slab_ref[pl.ds(at, BLK), :]
    for m in range(NB):
        turned_ref[:, m * BLK : (m + 1) * BLK] = table_ref[m * BLK : (m + 1) * BLK, :].T


def pool_body(first, *refs):
    if first:
        order_ref, own_ref, slab_ref, matrix_ref, out_ref, table_ref, turned_ref = refs

        @pl.when(pl.program_id(0) == 0)
        def _():
            merge(order_ref, own_ref, slab_ref, table_ref, turned_ref)
    else:
        turned_ref, matrix_ref, out_ref = refs
    join = matrix_ref.shape[0]
    right = jnp.concatenate([matrix_ref[q] for q in range(join)], axis=1)
    got = jnp.dot(turned_ref[...], right, preferred_element_type=jnp.float32)
    got = got.T.astype(jnp.bfloat16)
    for q in range(join):
        out_ref[q] = got[q * BLK : (q + 1) * BLK, :]


def pool(source, matrix, first, join=4):
    groups = matrix.shape[0]
    whole = lambda *shape: pl.BlockSpec(shape, lambda i: (0, 0))
    turned = whole(E, NB * BLK)
    ins = [SMEM, whole(R * BLK, E), whole(SLAB * BLK, E)] if first else [turned]
    outs = [pl.BlockSpec((join, BLK, E), lambda i: (i, 0, 0))]
    shapes = [jax.ShapeDtypeStruct((groups, BLK, E), jnp.bfloat16)]
    if first:
        outs += [whole(NB * BLK, E), turned]
        shapes += [
            jax.ShapeDtypeStruct((NB * BLK, E), jnp.bfloat16),
            jax.ShapeDtypeStruct((E, NB * BLK), jnp.bfloat16),
        ]
    return pl.pallas_call(
        functools.partial(pool_body, first),
        grid=(groups // join,),
        in_specs=ins + [pl.BlockSpec((join, NB * BLK, BLK), lambda i: (i, 0, 0))],
        out_specs=outs,
        out_shape=shapes,
        cost_estimate=pl.CostEstimate(
            flops=2 * matrix.size * E, bytes_accessed=matrix.size * 2, transcendentals=0
        ),
        name="pool",
    )(*source, matrix)


def layer_body(pair, start, *refs):
    if start:
        hid_before, fan_ref, top_hbm, cot_ref, hid_ref, out_ref, top_ref, sum_ref, pre_ref, sem = refs
    else:
        fan_ref, top_hbm, cot_ref, hid_ref, out_ref, top_ref, sum_ref, pre_ref, sem = refs
    fan, rows, _ = fan_ref.shape
    wide = pair * E
    steps = fan // pair

    def fetch(p):
        span = pl.ds(p * wide, wide)
        return pltpu.make_async_copy(top_hbm.at[span, :], top_ref.at[span, :], sem.at[p])

    for p in range(steps):
        fetch(p).start()
    if start:
        hid_ref[0:start, :] = hid_before[...]
    for p in range(steps):
        left = jnp.concatenate([fan_ref[p * pair + q] for q in range(pair)], axis=1)
        fetch(p).wait()
        part = jnp.dot(left, top_ref[p * wide : (p + 1) * wide, :], preferred_element_type=jnp.float32)
        if p == 0:
            sum_ref[...] = part
        else:
            sum_ref[...] += part
    preact = sum_ref[...]
    gate = jax.nn.sigmoid(preact)
    hid_ref[start : start + rows, :] = (preact * gate).astype(jnp.bfloat16)
    slope = gate * (1.0 + preact * (1.0 - gate))
    cot = cot_ref[start : start + rows, :].astype(jnp.float32)
    pre_ref[...] = (cot * slope).astype(jnp.bfloat16)
    for p in range(steps):
        back = lax.dot_general(
            pre_ref[...],
            top_ref[p * wide : (p + 1) * wide, :],
            (((1,), (1,)), ((), ())),
            preferred_element_type=jnp.float32,
        ).astype(jnp.bfloat16)
        for q in range(pair):
            out_ref[p * pair + q] = back[:, q * E : (q + 1) * E]


def layer(fan, top_weight, cotangent, before=(), pair=2):
    tables, rows, _ = fan.shape
    hidden = top_weight.shape[1]
    start = before[0].shape[0] if before else 0
    return pl.pallas_call(
        functools.partial(layer_body, pair, start),
        in_specs=[VMEM] * len(before) + [VMEM, ANY, VMEM],
        out_specs=[VMEM, VMEM],
        out_shape=[
            jax.ShapeDtypeStruct((start + rows, hidden), jnp.bfloat16),
            jax.ShapeDtypeStruct((tables, rows, E), jnp.bfloat16),
        ],
        scratch_shapes=[
            pltpu.VMEM(top_weight.shape, jnp.bfloat16),
            pltpu.VMEM((rows, hidden), jnp.float32),
            pltpu.VMEM((rows, hidden), jnp.bfloat16),
            pltpu.SemaphoreType.DMA((tables // pair,)),
        ],
        cost_estimate=pl.CostEstimate(
            flops=4 * rows * top_weight.size, bytes_accessed=rows * hidden * 6, transcendentals=rows * hidden
        ),
        name="layer",
    )(*before, fan, top_weight, cotangent)


def grad_body(more, *refs):
    if more:
        before_ref, matrix_ref, grad_ref, out_ref = refs
    else:
        matrix_ref, grad_ref, out_ref = refs
    left = jnp.concatenate([matrix_ref[q] for q in range(matrix_ref.shape[0])], axis=1)
    total = jnp.dot(left, grad_ref[...], preferred_element_type=jnp.float32)
    if more:
        total = total + before_ref[...]
    out_ref[...] = total.astype(out_ref.dtype)


def grad(matrix, pooled_grad, before=(), tile=256):
    groups = matrix.shape[0]
    block = pl.BlockSpec((tile, E), lambda i: (i, 0))
    return pl.pallas_call(
        functools.partial(grad_body, bool(before)),
        grid=(NB * BLK // tile,),
        in_specs=[block] * len(before)
        + [
            pl.BlockSpec((groups, tile, BLK), lambda i: (0, i, 0)),
            pl.BlockSpec((groups * BLK, E), lambda i: (0, 0)),
        ],
        out_specs=block,
        out_shape=jax.ShapeDtypeStruct((NB * BLK, E), jnp.bfloat16 if before else jnp.float32),
        cost_estimate=pl.CostEstimate(
            flops=2 * matrix.size * E, bytes_accessed=matrix.size * 2, transcendentals=0
        ),
        name="grad",
    )(*before, matrix, pooled_grad)


def everyone(block, axis):
    fan = lax.axis_size(axis)
    copies = jnp.broadcast_to(block[None], (fan,) + block.shape)
    return lax.all_to_all(copies, axis, split_axis=0, concat_axis=0, tiled=True)


def swap(blocks, axis):
    return lax.all_to_all(blocks, axis, split_axis=0, concat_axis=0, tiled=True)


def shards(
    own_table,
    own_accum,
    sectioned_rows,
    sectioned_accum,
    fold_pairs,
    slab_ids,
    bag_blocks,
    bag_counts,
    bag_weights,
    top_weight,
    hidden_grad,
):
    parts = lax.axis_size("dp")
    partner = fold_pairs[lax.axis_index("table")]
    block_order = slab_ids[partner]
    piece = lax.dynamic_index_in_dim(sectioned_rows, partner, 0, keepdims=False)
    slab_rows = everyone(piece, "dp").reshape(SLAB * BLK, E)
    bag_total = bag_blocks.shape[0]
    blocks = bag_blocks[:, 0, :].T
    counts = bag_counts.reshape(1, bag_total)
    even = spread(blocks, counts, bag_weights, 0)
    pooled, table_rows, turned = pool((block_order, own_table, slab_rows), even, True)
    pooled, blocks = lax.optimization_barrier((pooled, blocks))
    fan_even = swap(pooled, "table")
    odd = spread(blocks, counts, bag_weights, 1)
    (pooled,) = pool((turned,), odd, False)
    fan_odd = swap(pooled, "table")
    hidden, back = layer(fan_even, top_weight, hidden_grad)
    back_even = swap(back, "table")
    hidden, back = layer(fan_odd, top_weight, hidden_grad, (hidden,))
    back_odd = swap(back, "table")
    row_grad = grad(even, back_even.reshape(bag_total // 2, E))
    row_grad = grad(odd, back_odd.reshape(bag_total // 2, E), (row_grad,))

    share = NB * BLK // parts
    start = lax.axis_index("dp") * share
    state = lax.dynamic_index_in_dim(sectioned_accum, partner, 0, keepdims=False)
    folded_state = jnp.take(state.reshape(SLAB, BLK), block_order, axis=0).reshape(SLAB * BLK)
    merged_accum = jnp.concatenate([own_accum, folded_state], axis=0)
    accum = lax.dynamic_slice_in_dim(merged_accum, start, share, 0)
    rows = lax.dynamic_slice_in_dim(table_rows, start, share, 0)
    received = swap(row_grad.reshape(parts, share, E), "dp")
    total = jnp.sum(received.astype(jnp.float32), axis=0)
    new_accum = accum + jnp.mean(total * total, axis=1)
    step_size = learn_rate / (jnp.sqrt(new_accum) + ada_epsilon)
    new_rows = (rows.astype(jnp.float32) - step_size[:, None] * total).astype(jnp.bfloat16)
    new_table = everyone(new_rows, "dp").reshape(NB * BLK, E)
    return (new_table, new_accum, hidden)


def solution(mesh):
    placed = (
        P("table", None),
        P("table"),
        P(None, "dp", None),
        P(),
        P(),
        P(),
        P("dp", "table", None),
        P("dp", "table"),
        P("dp", "table", None, None),
        P(),
        P(("dp", "table"), None),
    )
    return jax.shard_map(
        shards,
        mesh=mesh,
        in_specs=placed,
        out_specs=(P("table", None), P(("table", "dp")), P(("dp", "table"), None)),
        check_vma=False,
    )
```

```python
import functools

import jax
import jax.numpy as jnp
from jax import lax
from jax.experimental import pallas as pl
from jax.experimental.pallas import tpu as pltpu
from jax.sharding import PartitionSpec as P

E = 128
BLK = 128
R = 10
SLAB = 6
K = 4
NB = R + SLAB
TILE = 16
WIDE = K * BLK

learn_rate = 0.5
ada_epsilon = 1e-08

ANY = pl.BlockSpec(memory_space=pl.ANY)
HBM = pl.BlockSpec(memory_space=pltpu.HBM)
SMEM = pl.BlockSpec(memory_space=pltpu.SMEM)
VMEM = pl.BlockSpec(memory_space=pltpu.VMEM)


def fill_perm(perm_ref):
    row = lax.broadcasted_iota(jnp.int32, (WIDE, BLK), 0)
    lane = lax.broadcasted_iota(jnp.int32, (WIDE, BLK), 1)
    for k in range(K):
        perm_ref[k] = jnp.where(row == lane * K + k, 1.0, 0.0).astype(jnp.bfloat16)


def turn(window, at, perm_ref, part_ref):
    turned = jnp.concatenate([window[pl.ds(at + BLK * n, BLK), :].T for n in range(K)], axis=1)
    for k in range(0, K, 2):
        right = jnp.concatenate([perm_ref[k], perm_ref[k + 1]], axis=1)
        got = jnp.dot(turned, right, preferred_element_type=jnp.float32).astype(jnp.bfloat16)
        part_ref[k] = got[:, :BLK]
        part_ref[k + 1] = got[:, BLK:]


def place(block_ref, count_ref, base, part_ref, out_ref, at):
    blocks = block_ref[:, pl.ds(base, BLK)]
    counts = count_ref[:, pl.ds(base, BLK)]
    names = []
    for k in range(K):
        name = jnp.where(counts > k, blocks[k : k + 1, :], NB).astype(jnp.float32)
        names.append(jnp.broadcast_to(name, (TILE, BLK)).astype(jnp.bfloat16))
    for m in range(NB):
        hits = [names[k] == jnp.bfloat16(m) for k in range(K)]
        for s in range(0, BLK, TILE):
            value = jnp.zeros((TILE, BLK), jnp.bfloat16)
            for k in range(K):
                value = jnp.where(hits[k], part_ref[k, s : s + TILE, :], value)
            out_ref[at, m * BLK + s : m * BLK + s + TILE, :] = value


def fetches(source, base, target, sem, pieces):
    size = target.shape[0] // pieces

    def piece(n):
        return pltpu.make_async_copy(
            source.at[pl.ds(base + n * size, size)], target.at[pl.ds(n * size, size)], sem.at[n]
        )

    return piece


def pair_out(matrix, out_hbm, sem, pair):
    span = pl.ds(pl.multiple_of(pair * 2, 2), 2)
    return pltpu.make_async_copy(matrix.at[span], out_hbm.at[span], sem.at[pair])


def early_body(block_ref, count_ref, weight_hbm, out_hbm, window, perm_ref, even_ref, odd_ref, matrix, in_sem, out_sem):
    groups = matrix.shape[0]
    pairs = groups // 2
    fetch = fetches(weight_hbm, 0, window, in_sem, pairs)
    for n in range(pairs):
        fetch(n).start()
    fill_perm(perm_ref)

    def put(group, part_ref):
        place(block_ref, count_ref, pl.multiple_of(group * BLK, BLK), part_ref, matrix, group)

    fetch(0).wait()
    turn(window, 0, perm_ref, even_ref)

    def step(pair, carry):
        group = 2 * pair
        turn(window, pl.multiple_of((group + 1) * WIDE, WIDE), perm_ref, odd_ref)
        put(group, even_ref)

        @pl.when(pair + 1 < pairs)
        def _():
            fetch(pair + 1).wait()

        turn(window, pl.multiple_of(lax.rem(group + 2, groups) * WIDE, WIDE), perm_ref, even_ref)
        put(group + 1, odd_ref)
        pair_out(matrix, out_hbm, out_sem, pair).start()
        return carry

    lax.fori_loop(0, pairs, step, 0)
    for pair in range(pairs):
        pair_out(matrix, out_hbm, out_sem, pair).wait()


def build_scratch(groups):
    return [
        pltpu.VMEM((groups * WIDE, BLK), jnp.bfloat16),
        pltpu.VMEM((K, WIDE, BLK), jnp.bfloat16),
        pltpu.VMEM((K, BLK, BLK), jnp.bfloat16),
        pltpu.VMEM((K, BLK, BLK), jnp.bfloat16),
    ]


def early(blocks, counts, weights, groups):
    return pl.pallas_call(
        early_body,
        in_specs=[VMEM, VMEM, HBM],
        out_specs=ANY,
        out_shape=jax.ShapeDtypeStruct((groups, NB * BLK, BLK), jnp.bfloat16),
        scratch_shapes=build_scratch(groups)
        + [
            pltpu.VMEM((groups, NB * BLK, BLK), jnp.bfloat16),
            pltpu.SemaphoreType.DMA((groups // 2,)),
            pltpu.SemaphoreType.DMA((groups // 2,)),
        ],
        cost_estimate=pl.CostEstimate(
            flops=groups * BLK * NB * BLK * 256, bytes_accessed=groups * WIDE * BLK * 10, transcendentals=0
        ),
        name="early",
    )(blocks, counts, weights)


def pool_body(
    order_ref, block_ref, count_ref, own_ref, slab_ref, weight_hbm, early_hbm,
    out_hbm, matrix, share_ref,
    window, perm_ref, even_ref, odd_ref, table_ref, turned_ref, pooled, in_sem, before_sem, pool_sem,
):
    early_groups = early_hbm.shape[0]
    late_groups = matrix.shape[0] - early_groups
    pairs = late_groups // 2
    fetch = fetches(weight_hbm, early_groups * WIDE, window, in_sem, pairs)
    again = fetches(early_hbm, 0, matrix.at[pl.ds(0, early_groups)], before_sem, early_groups // 2)
    for n in range(max(pairs, early_groups // 2)):
        if n < pairs:
            fetch(n).start()
        if n < early_groups // 2:
            again(n).start()
    fill_perm(perm_ref)
    table_ref[0 : R * BLK, :] = own_ref[...]
    for j in range(SLAB):
        at = pl.multiple_of(order_ref[j] * BLK, BLK)
        table_ref[(R + j) * BLK : (R + j + 1) * BLK, :] = slab_ref[pl.ds(at, BLK), :]
    for m in range(NB):
        turned_ref[:, m * BLK : (m + 1) * BLK] = table_ref[m * BLK : (m + 1) * BLK, :].T
    share = share_ref.shape[0]
    share_ref[...] = table_ref[pl.ds(pl.multiple_of(lax.axis_index("dp") * share, share), share), :]

    def send(first, count):
        span = pl.ds(first * BLK, count * BLK)
        return pltpu.make_async_copy(pooled.at[span, :], out_hbm.at[span, :], pool_sem)

    def sums(at, count):
        right = jnp.concatenate([matrix[at + q] for q in range(count)], axis=1)
        got = jnp.dot(turned_ref[...], right, preferred_element_type=jnp.float32)
        pooled[pl.ds(pl.multiple_of(at * BLK, BLK), count * BLK), :] = got.T.astype(jnp.bfloat16)

    def put(group, part_ref):
        base = pl.multiple_of((early_groups + group) * BLK, BLK)
        place(block_ref, count_ref, base, part_ref, matrix, early_groups + group)

    fetch(0).wait()
    turn(window, 0, perm_ref, even_ref)

    def step(pair, carry):
        group = 2 * pair
        turn(window, pl.multiple_of((group + 1) * WIDE, WIDE), perm_ref, odd_ref)
        put(group, even_ref)

        @pl.when(pair + 1 < pairs)
        def _():
            fetch(pair + 1).wait()

        turn(window, pl.multiple_of(lax.rem(group + 2, late_groups) * WIDE, WIDE), perm_ref, even_ref)
        put(group + 1, odd_ref)
        return carry

    lax.fori_loop(0, pairs, step, 0)
    for n in range(early_groups // 2):
        again(n).wait()

    def rest(n, carry):
        sums(4 * n, 4)
        return carry

    half = matrix.shape[0] // 2
    lax.fori_loop(0, half // 4, rest, 0)
    send(0, half).start()
    lax.fori_loop(half // 4, half // 2, rest, 0)
    send(half, half).start()
    send(0, 2 * half).wait()


def pool(order, blocks, counts, own, slab, weights, before, share):
    bags = blocks.shape[1]
    groups = bags // BLK
    late = groups - before.shape[0]
    return pl.pallas_call(
        pool_body,
        in_specs=[SMEM, VMEM, VMEM, VMEM, VMEM, HBM, HBM],
        out_specs=[ANY, VMEM, VMEM],
        out_shape=[
            jax.ShapeDtypeStruct((bags, E), jnp.bfloat16),
            pltpu.VMEM((groups, NB * BLK, BLK), jnp.bfloat16),
            jax.ShapeDtypeStruct((share, E), jnp.bfloat16),
        ],
        scratch_shapes=build_scratch(late)
        + [
            pltpu.VMEM((NB * BLK, E), jnp.bfloat16),
            pltpu.VMEM((E, NB * BLK), jnp.bfloat16),
            pltpu.VMEM((bags, E), jnp.bfloat16),
            pltpu.SemaphoreType.DMA((late // 2,)),
            pltpu.SemaphoreType.DMA((before.shape[0] // 2,)),
            pltpu.SemaphoreType.DMA,
        ],
        cost_estimate=pl.CostEstimate(
            flops=2 * bags * NB * BLK * E, bytes_accessed=bags * NB * BLK * 2, transcendentals=0
        ),
        compiler_params=pltpu.CompilerParams(vmem_limit_bytes=44 << 20),
        name="pool",
    )(order, blocks, counts, own, slab, weights, before)


def layer_body(pair, fan_hbm, top_hbm, cot_hbm, hid_hbm, out_hbm, fan_ref, top_ref, cot_ref, hid_ref, out_ref, sum_ref, pre_ref, fan_sem, top_sem, cot_sem, out_sem):
    fan, rows, _ = fan_ref.shape
    wide = pair * E
    steps = fan // pair
    fetch_fan = fetches(fan_hbm, 0, fan_ref, fan_sem, steps)
    fetch_top = fetches(top_hbm, 0, top_ref, top_sem, steps)
    fetch_cot = pltpu.make_async_copy(cot_hbm, cot_ref, cot_sem)
    send_hid = pltpu.make_async_copy(hid_ref, hid_hbm, cot_sem)

    def send_out(p):
        span = pl.ds(p * pair, pair)
        return pltpu.make_async_copy(out_ref.at[span], out_hbm.at[span], out_sem)

    for p in range(steps):
        fetch_fan(p).start()
        fetch_top(p).start()
    fetch_cot.start()
    for p in range(steps):
        fetch_fan(p).wait()
        left = jnp.concatenate([fan_ref[p * pair + q] for q in range(pair)], axis=1)
        fetch_top(p).wait()
        part = jnp.dot(left, top_ref[p * wide : (p + 1) * wide, :], preferred_element_type=jnp.float32)
        if p == 0:
            sum_ref[...] = part
        else:
            sum_ref[...] += part
    fetch_cot.wait()
    preact = sum_ref[...]
    gate = jax.nn.sigmoid(preact)
    hid_ref[...] = (preact * gate).astype(jnp.bfloat16)
    send_hid.start()
    slope = gate * (1.0 + preact * (1.0 - gate))
    pre_ref[...] = (cot_ref[...].astype(jnp.float32) * slope).astype(jnp.bfloat16)
    for p in range(steps):
        back = lax.dot_general(
            pre_ref[...],
            top_ref[p * wide : (p + 1) * wide, :],
            (((1,), (1,)), ((), ())),
            preferred_element_type=jnp.float32,
        ).astype(jnp.bfloat16)
        for q in range(pair):
            out_ref[p * pair + q] = back[:, q * E : (q + 1) * E]
        send_out(p).start()
    send_hid.wait()
    pltpu.make_async_copy(out_ref, out_hbm, out_sem).wait()


def layer(fan, top_weight, cotangent, pair=2):
    tables, rows, _ = fan.shape
    hidden = top_weight.shape[1]
    steps = tables // pair
    return pl.pallas_call(
        functools.partial(layer_body, pair),
        in_specs=[ANY, HBM, HBM],
        out_specs=[HBM, ANY],
        out_shape=[
            jax.ShapeDtypeStruct((rows, hidden), jnp.bfloat16),
            jax.ShapeDtypeStruct((tables, rows, E), jnp.bfloat16),
        ],
        scratch_shapes=[
            pltpu.VMEM(fan.shape, jnp.bfloat16),
            pltpu.VMEM(top_weight.shape, jnp.bfloat16),
            pltpu.VMEM((rows, hidden), jnp.bfloat16),
            pltpu.VMEM((rows, hidden), jnp.bfloat16),
            pltpu.VMEM(fan.shape, jnp.bfloat16),
            pltpu.VMEM((rows, hidden), jnp.float32),
            pltpu.VMEM((rows, hidden), jnp.bfloat16),
            pltpu.SemaphoreType.DMA((steps,)),
            pltpu.SemaphoreType.DMA((steps,)),
            pltpu.SemaphoreType.DMA,
            pltpu.SemaphoreType.DMA,
        ],
        cost_estimate=pl.CostEstimate(
            flops=4 * rows * top_weight.size, bytes_accessed=rows * hidden * 6, transcendentals=rows * hidden
        ),
        compiler_params=pltpu.CompilerParams(vmem_limit_bytes=45 << 20),
        name="layer",
    )(fan, top_weight, cotangent)


def grad_body(tile, matrix, grad_ref, out_hbm, out_ref, sem):
    def send(n):
        span = pl.ds(pl.multiple_of(n * tile, tile), tile)
        return pltpu.make_async_copy(out_ref.at[span, :], out_hbm.at[span, :], sem)

    def rows(n, carry):
        span = pl.ds(pl.multiple_of(n * tile, tile), tile)
        left = jnp.concatenate([matrix[q, span, :] for q in range(matrix.shape[0])], axis=1)
        total = jnp.dot(left, grad_ref[...], preferred_element_type=jnp.float32)
        out_ref[span, :] = total.astype(jnp.bfloat16)
        send(n).start()
        return carry

    lax.fori_loop(0, NB * BLK // tile, rows, 0)
    pltpu.make_async_copy(out_ref, out_hbm, sem).wait()


def grad(matrix, pooled_grad, tile=512):
    return pl.pallas_call(
        functools.partial(grad_body, tile),
        in_specs=[VMEM, VMEM],
        out_specs=ANY,
        out_shape=jax.ShapeDtypeStruct((NB * BLK, E), jnp.bfloat16),
        scratch_shapes=[pltpu.VMEM((NB * BLK, E), jnp.bfloat16), pltpu.SemaphoreType.DMA],
        cost_estimate=pl.CostEstimate(
            flops=2 * pooled_grad.size * NB * BLK, bytes_accessed=pooled_grad.size * 4, transcendentals=0
        ),
        compiler_params=pltpu.CompilerParams(vmem_limit_bytes=8 << 20),
        name="grad",
    )(matrix, pooled_grad)


def pick_body(pair_ref, ids_ref, sect_ref, state_ref, accum_ref, copies_ref, order_ref, out_ref):
    partner = pair_ref[lax.axis_index("table")]
    for n in range(copies_ref.shape[0]):
        copies_ref[n] = sect_ref[partner]
    for j in range(SLAB):
        order_ref[j] = ids_ref[j, partner]
    count = out_ref.shape[0]
    for n in range(count):
        block = lax.axis_index("dp") * count + n
        own = accum_ref[pl.ds(jnp.minimum(block, R - 1), 1), :]
        fold = pl.multiple_of(ids_ref[jnp.maximum(block - R, 0), partner] * BLK, BLK)
        states = state_ref[:, pl.ds(fold, BLK)]
        mine = lax.broadcasted_iota(jnp.int32, states.shape, 0) == partner
        other = jnp.sum(jnp.where(mine, states, 0.0), axis=0, keepdims=True)
        out_ref[n : n + 1, :] = jnp.where(block < R, own, other)


def pick(fold_pairs, slab_ids, sectioned_rows, sectioned_accum, own_accum, parts):
    _, size, width = sectioned_rows.shape
    return pl.pallas_call(
        pick_body,
        in_specs=[SMEM, SMEM, VMEM, VMEM, VMEM],
        out_specs=[VMEM, SMEM, VMEM],
        out_shape=[
            jax.ShapeDtypeStruct((parts, size, width), jnp.bfloat16),
            jax.ShapeDtypeStruct((SLAB,), jnp.int32),
            jax.ShapeDtypeStruct((NB // parts, BLK), jnp.float32),
        ],
        name="pick",
    )(fold_pairs, slab_ids.T, sectioned_rows, sectioned_accum, own_accum.reshape(R, BLK))


def update_body(part_ref, row_ref, accum_ref, copies_ref, out_ref):
    for n in range(accum_ref.shape[0]):
        span = slice(n * BLK, (n + 1) * BLK)
        total = part_ref[0, span, :].astype(jnp.float32)
        for q in range(1, part_ref.shape[0]):
            total = total + part_ref[q, span, :].astype(jnp.float32)
        before = jnp.broadcast_to(accum_ref[n : n + 1, :], (BLK, BLK)).T
        accum = before + jnp.mean(total * total, axis=1, keepdims=True)
        out_ref[n : n + 1, :] = accum.T[0:1, :]
        step_size = learn_rate / (jnp.sqrt(accum) + ada_epsilon)
        rows = (row_ref[span, :].astype(jnp.float32) - step_size * total).astype(jnp.bfloat16)
        for q in range(copies_ref.shape[0]):
            copies_ref[q, span, :] = rows


def update(received, rows, accum):
    return pl.pallas_call(
        update_body,
        in_specs=[VMEM, VMEM, VMEM],
        out_specs=[VMEM, VMEM],
        out_shape=[
            jax.ShapeDtypeStruct(received.shape, jnp.bfloat16),
            jax.ShapeDtypeStruct(accum.shape, jnp.float32),
        ],
        name="update",
    )(received, rows, accum)


def swap(blocks, axis):
    return lax.all_to_all(blocks, axis, split_axis=0, concat_axis=0, tiled=True)


def shards(
    own_table,
    own_accum,
    sectioned_rows,
    sectioned_accum,
    fold_pairs,
    slab_ids,
    bag_blocks,
    bag_counts,
    bag_weights,
    top_weight,
    hidden_grad,
):
    tables = lax.axis_size("table")
    parts = lax.axis_size("dp")
    share = NB * BLK // parts
    bag_total = bag_blocks.shape[0]
    copies, order, accum = pick(fold_pairs, slab_ids, sectioned_rows, sectioned_accum, own_accum, parts)
    slab_rows = swap(copies, "dp").reshape(SLAB * BLK, E)
    blocks = bag_blocks[:, 0, :].T
    counts = bag_counts.reshape(1, bag_total)
    weights = bag_weights.reshape(bag_total * K, BLK)
    before = early(blocks, counts, weights, bag_total // (2 * BLK))
    pooled, matrix, rows = pool(order, blocks, counts, own_table, slab_rows, weights, before, share)
    fan = swap(pooled.reshape(tables, bag_total // tables, E), "table")
    hidden, back = layer(fan, top_weight, hidden_grad)
    row_grad = grad(matrix, swap(back, "table").reshape(bag_total, E))
    received = swap(row_grad.reshape(parts, share, E), "dp")
    copies, accum = update(received, rows, accum)
    new_table = swap(copies, "dp").reshape(NB * BLK, E)
    return (new_table, accum.reshape(share), hidden)


def solution(mesh):
    placed = (
        P("table", None),
        P("table"),
        P(None, "dp", None),
        P(),
        P(),
        P(),
        P("dp", "table", None),
        P("dp", "table"),
        P("dp", "table", None, None),
        P(),
        P(("dp", "table"), None),
    )
    return jax.shard_map(
        shards,
        mesh=mesh,
        in_specs=placed,
        out_specs=(P("table", None), P(("table", "dp")), P(("dp", "table"), None)),
        check_vma=False,
    )
```

```python
import functools

import jax
import jax.numpy as jnp
from jax import lax
from jax.experimental import pallas as pl
from jax.experimental.pallas import tpu as pltpu
from jax.sharding import PartitionSpec as P

E = 128
BLK = 128
R = 10
SLAB = 6
K = 4
NB = R + SLAB
TILE = 16
WIDE = K * BLK

learn_rate = 0.5
ada_epsilon = 1e-08

ANY = pl.BlockSpec(memory_space=pl.ANY)
HBM = pl.BlockSpec(memory_space=pltpu.HBM)
SMEM = pl.BlockSpec(memory_space=pltpu.SMEM)
VMEM = pl.BlockSpec(memory_space=pltpu.VMEM)


def fill_perm(perm_ref):
    row = lax.broadcasted_iota(jnp.int32, (WIDE, BLK), 0)
    lane = lax.broadcasted_iota(jnp.int32, (WIDE, BLK), 1)
    for k in range(K):
        perm_ref[k] = jnp.where(row == lane * K + k, 1.0, 0.0).astype(jnp.bfloat16)


def turn(window, at, perm_ref, part_ref):
    turned = jnp.concatenate([window[pl.ds(at + BLK * n, BLK), :].T for n in range(K)], axis=1)
    for k in range(0, K, 2):
        right = jnp.concatenate([perm_ref[k], perm_ref[k + 1]], axis=1)
        got = jnp.dot(turned, right, preferred_element_type=jnp.float32).astype(jnp.bfloat16)
        part_ref[k] = got[:, :BLK]
        part_ref[k + 1] = got[:, BLK:]


def place(block_ref, count_ref, base, part_ref, out_ref, at):
    blocks = block_ref[:, pl.ds(base, BLK)]
    counts = count_ref[:, pl.ds(base, BLK)]
    names = []
    for k in range(K):
        name = jnp.where(counts > k, blocks[k : k + 1, :], NB).astype(jnp.float32)
        names.append(jnp.broadcast_to(name, (TILE, BLK)).astype(jnp.bfloat16))
    for m in range(NB):
        hits = [names[k] == jnp.bfloat16(m) for k in range(K)]
        for s in range(0, BLK, TILE):
            value = jnp.zeros((TILE, BLK), jnp.bfloat16)
            for k in range(K):
                value = jnp.where(hits[k], part_ref[k, s : s + TILE, :], value)
            out_ref[at, m * BLK + s : m * BLK + s + TILE, :] = value


def fetches(source, base, target, sem, pieces):
    size = target.shape[0] // pieces

    def piece(n):
        return pltpu.make_async_copy(
            source.at[pl.ds(base + n * size, size)], target.at[pl.ds(n * size, size)], sem.at[n]
        )

    return piece


def pair_out(matrix, out_hbm, sem, pair):
    span = pl.ds(pl.multiple_of(pair * 2, 2), 2)
    return pltpu.make_async_copy(matrix.at[span], out_hbm.at[span], sem.at[pair])


def early_body(block_ref, count_ref, weight_hbm, out_hbm, window, perm_ref, even_ref, odd_ref, matrix, in_sem, out_sem):
    groups = matrix.shape[0]
    pairs = groups // 2
    fetch = fetches(weight_hbm, 0, window, in_sem, pairs)
    for n in range(pairs):
        fetch(n).start()
    fill_perm(perm_ref)

    def put(pair):
        for part_ref, group in ((even_ref, 2 * pair), (odd_ref, 2 * pair + 1)):
            place(block_ref, count_ref, pl.multiple_of(group * BLK, BLK), part_ref, matrix, group)

    def ready(pair):
        turn(window, pl.multiple_of(2 * pair * WIDE, WIDE), perm_ref, even_ref)
        turn(window, pl.multiple_of((2 * pair + 1) * WIDE, WIDE), perm_ref, odd_ref)

    def step(pair, carry):
        fetch(pair + 1).wait()
        put(pair)
        ready(pair + 1)
        pair_out(matrix, out_hbm, out_sem, pair).start()
        return carry

    fetch(0).wait()
    ready(0)
    lax.fori_loop(0, pairs - 1, step, 0)
    put(pairs - 1)
    pair_out(matrix, out_hbm, out_sem, pairs - 1).start()
    for pair in range(pairs):
        pair_out(matrix, out_hbm, out_sem, pair).wait()


def build_scratch(groups):
    return [
        pltpu.VMEM((groups * WIDE, BLK), jnp.bfloat16),
        pltpu.VMEM((K, WIDE, BLK), jnp.bfloat16),
        pltpu.VMEM((K, BLK, BLK), jnp.bfloat16),
        pltpu.VMEM((K, BLK, BLK), jnp.bfloat16),
    ]


def early(blocks, counts, weights, groups):
    return pl.pallas_call(
        early_body,
        in_specs=[VMEM, VMEM, HBM],
        out_specs=ANY,
        out_shape=jax.ShapeDtypeStruct((groups, NB * BLK, BLK), jnp.bfloat16),
        scratch_shapes=build_scratch(groups)
        + [
            pltpu.VMEM((groups, NB * BLK, BLK), jnp.bfloat16),
            pltpu.SemaphoreType.DMA((groups // 2,)),
            pltpu.SemaphoreType.DMA((groups // 2,)),
        ],
        cost_estimate=pl.CostEstimate(
            flops=groups * BLK * NB * BLK * 256, bytes_accessed=groups * WIDE * BLK * 10, transcendentals=0
        ),
        name="early",
    )(blocks, counts, weights)


def pool_body(
    order_ref, block_ref, count_ref, own_ref, slab_ref, weight_hbm, early_hbm,
    out_hbm, before, matrix, share_ref,
    window, perm_ref, even_ref, odd_ref, table_ref, turned_ref, pooled, in_sem, before_sem, pool_sem,
):
    early_groups = early_hbm.shape[0]
    late_groups = matrix.shape[0]
    pairs = late_groups // 2
    fetch = fetches(weight_hbm, early_groups * WIDE, window, in_sem, pairs)
    again = fetches(early_hbm, 0, before, before_sem, pairs)
    for n in range(pairs):
        fetch(n).start()
        again(n).start()
    fill_perm(perm_ref)
    table_ref[0 : R * BLK, :] = own_ref[...]
    for j in range(SLAB):
        at = pl.multiple_of(order_ref[j] * BLK, BLK)
        table_ref[(R + j) * BLK : (R + j + 1) * BLK, :] = slab_ref[pl.ds(at, BLK), :]
    for m in range(NB):
        turned_ref[:, m * BLK : (m + 1) * BLK] = table_ref[m * BLK : (m + 1) * BLK, :].T
    share = share_ref.shape[0]
    share_ref[...] = table_ref[pl.ds(pl.multiple_of(lax.axis_index("dp") * share, share), share), :]

    def send(first, count):
        span = pl.ds(first * BLK, count * BLK)
        return pltpu.make_async_copy(pooled.at[span, :], out_hbm.at[span, :], pool_sem)

    def sums(source, at, count, to):
        right = jnp.concatenate([source[at + q] for q in range(count)], axis=1)
        got = jnp.dot(turned_ref[...], right, preferred_element_type=jnp.float32)
        pooled[pl.ds(pl.multiple_of(to * BLK, BLK), count * BLK), :] = got.T.astype(jnp.bfloat16)

    def put(pair):
        for part_ref, group in ((even_ref, 2 * pair), (odd_ref, 2 * pair + 1)):
            base = pl.multiple_of((early_groups + group) * BLK, BLK)
            place(block_ref, count_ref, base, part_ref, matrix, group)

    def ready(pair):
        turn(window, pl.multiple_of(2 * pair * WIDE, WIDE), perm_ref, even_ref)
        turn(window, pl.multiple_of((2 * pair + 1) * WIDE, WIDE), perm_ref, odd_ref)

    per = early_groups // pairs

    def step(pair, carry):
        fetch(pair + 1).wait()
        again(pair).wait()
        put(pair)
        sums(before, per * pair, per, per * pair)
        ready(pair + 1)
        return carry

    fetch(0).wait()
    ready(0)
    lax.fori_loop(0, pairs - 1, step, 0)
    again(pairs - 1).wait()
    put(pairs - 1)
    sums(before, per * (pairs - 1), per, per * (pairs - 1))
    send(0, early_groups).start()

    def rest(n, carry):
        sums(matrix, 4 * n, 4, early_groups + 4 * n)
        return carry

    lax.fori_loop(0, late_groups // 4, rest, 0)
    send(early_groups, late_groups).start()
    send(0, early_groups + late_groups).wait()


def pool(order, blocks, counts, own, slab, weights, before, share):
    bags = blocks.shape[1]
    groups = bags // BLK
    late = groups - before.shape[0]
    return pl.pallas_call(
        pool_body,
        in_specs=[SMEM, VMEM, VMEM, VMEM, VMEM, HBM, HBM],
        out_specs=[ANY, VMEM, VMEM, VMEM],
        out_shape=[
            jax.ShapeDtypeStruct((bags, E), jnp.bfloat16),
            pltpu.VMEM(before.shape, jnp.bfloat16),
            pltpu.VMEM((late, NB * BLK, BLK), jnp.bfloat16),
            jax.ShapeDtypeStruct((share, E), jnp.bfloat16),
        ],
        scratch_shapes=build_scratch(late)
        + [
            pltpu.VMEM((NB * BLK, E), jnp.bfloat16),
            pltpu.VMEM((E, NB * BLK), jnp.bfloat16),
            pltpu.VMEM((bags, E), jnp.bfloat16),
            pltpu.SemaphoreType.DMA((late // 2,)),
            pltpu.SemaphoreType.DMA((late // 2,)),
            pltpu.SemaphoreType.DMA,
        ],
        cost_estimate=pl.CostEstimate(
            flops=2 * bags * NB * BLK * E, bytes_accessed=bags * NB * BLK * 2, transcendentals=0
        ),
        compiler_params=pltpu.CompilerParams(vmem_limit_bytes=40 << 20),
        name="pool",
    )(order, blocks, counts, own, slab, weights, before)


def layer_body(pair, fan_ref, top_ref, cot_ref, hid_hbm, out_ref, hid_ref, sum_ref, pre_ref, sem):
    fan, rows, _ = fan_ref.shape
    wide = pair * E
    steps = fan // pair
    send_hid = pltpu.make_async_copy(hid_ref, hid_hbm, sem)
    for p in range(steps):
        left = jnp.concatenate([fan_ref[p * pair + q] for q in range(pair)], axis=1)
        part = jnp.dot(left, top_ref[p * wide : (p + 1) * wide, :], preferred_element_type=jnp.float32)
        if p == 0:
            sum_ref[...] = part
        else:
            sum_ref[...] += part
    preact = sum_ref[...]
    gate = jax.nn.sigmoid(preact)
    hid_ref[...] = (preact * gate).astype(jnp.bfloat16)
    send_hid.start()
    slope = gate * (1.0 + preact * (1.0 - gate))
    pre_ref[...] = (cot_ref[...].astype(jnp.float32) * slope).astype(jnp.bfloat16)
    for p in range(steps):
        back = lax.dot_general(
            pre_ref[...],
            top_ref[p * wide : (p + 1) * wide, :],
            (((1,), (1,)), ((), ())),
            preferred_element_type=jnp.float32,
        ).astype(jnp.bfloat16)
        for q in range(pair):
            out_ref[p * pair + q] = back[:, q * E : (q + 1) * E]
    send_hid.wait()


def layer(fan, top_weight, cotangent, pair=4):
    tables, rows, _ = fan.shape
    hidden = top_weight.shape[1]
    return pl.pallas_call(
        functools.partial(layer_body, pair),
        in_specs=[VMEM, VMEM, VMEM],
        out_specs=[HBM, VMEM],
        out_shape=[
            jax.ShapeDtypeStruct((rows, hidden), jnp.bfloat16),
            jax.ShapeDtypeStruct((tables, rows, E), jnp.bfloat16),
        ],
        scratch_shapes=[
            pltpu.VMEM((rows, hidden), jnp.bfloat16),
            pltpu.VMEM((rows, hidden), jnp.float32),
            pltpu.VMEM((rows, hidden), jnp.bfloat16),
            pltpu.SemaphoreType.DMA,
        ],
        cost_estimate=pl.CostEstimate(
            flops=4 * rows * top_weight.size, bytes_accessed=rows * hidden * 6, transcendentals=rows * hidden
        ),
        compiler_params=pltpu.CompilerParams(vmem_limit_bytes=16 << 20),
        name="layer",
    )(fan, top_weight, cotangent)


def grad_body(tile, before, after, grad_ref, out_hbm, out_ref, sem):
    def send(n):
        span = pl.ds(pl.multiple_of(n * tile, tile), tile)
        return pltpu.make_async_copy(out_ref.at[span, :], out_hbm.at[span, :], sem)

    def rows(n, carry):
        span = pl.ds(pl.multiple_of(n * tile, tile), tile)
        left = [ref[q, span, :] for ref in (before, after) for q in range(ref.shape[0])]
        total = jnp.dot(jnp.concatenate(left, axis=1), grad_ref[...], preferred_element_type=jnp.float32)
        out_ref[span, :] = total.astype(jnp.bfloat16)
        send(n).start()
        return carry

    lax.fori_loop(0, NB * BLK // tile, rows, 0)
    pltpu.make_async_copy(out_ref, out_hbm, sem).wait()


def grad(before, after, pooled_grad, tile=512):
    return pl.pallas_call(
        functools.partial(grad_body, tile),
        in_specs=[VMEM, VMEM, VMEM],
        out_specs=ANY,
        out_shape=jax.ShapeDtypeStruct((NB * BLK, E), jnp.bfloat16),
        scratch_shapes=[pltpu.VMEM((NB * BLK, E), jnp.bfloat16), pltpu.SemaphoreType.DMA],
        cost_estimate=pl.CostEstimate(
            flops=2 * pooled_grad.size * NB * BLK, bytes_accessed=pooled_grad.size * 4, transcendentals=0
        ),
        compiler_params=pltpu.CompilerParams(vmem_limit_bytes=8 << 20),
        name="grad",
    )(before, after, pooled_grad)


def pick_body(pair_ref, ids_ref, sect_ref, state_ref, accum_ref, copies_ref, order_ref, out_ref):
    partner = pair_ref[lax.axis_index("table")]
    for n in range(copies_ref.shape[0]):
        copies_ref[n] = sect_ref[partner]
    for j in range(SLAB):
        order_ref[j] = ids_ref[j, partner]
    count = out_ref.shape[0]
    for n in range(count):
        block = lax.axis_index("dp") * count + n
        own = accum_ref[pl.ds(jnp.minimum(block, R - 1), 1), :]
        fold = pl.multiple_of(ids_ref[jnp.maximum(block - R, 0), partner] * BLK, BLK)
        states = state_ref[:, pl.ds(fold, BLK)]
        mine = lax.broadcasted_iota(jnp.int32, states.shape, 0) == partner
        other = jnp.sum(jnp.where(mine, states, 0.0), axis=0, keepdims=True)
        out_ref[n : n + 1, :] = jnp.where(block < R, own, other)


def pick(fold_pairs, slab_ids, sectioned_rows, sectioned_accum, own_accum, parts):
    _, size, width = sectioned_rows.shape
    return pl.pallas_call(
        pick_body,
        in_specs=[SMEM, SMEM, VMEM, VMEM, VMEM],
        out_specs=[VMEM, SMEM, VMEM],
        out_shape=[
            jax.ShapeDtypeStruct((parts, size, width), jnp.bfloat16),
            jax.ShapeDtypeStruct((SLAB,), jnp.int32),
            jax.ShapeDtypeStruct((NB // parts, BLK), jnp.float32),
        ],
        name="pick",
    )(fold_pairs, slab_ids.T, sectioned_rows, sectioned_accum, own_accum.reshape(R, BLK))


def update_body(part_ref, row_ref, accum_ref, copies_ref, out_ref):
    for n in range(accum_ref.shape[0]):
        span = slice(n * BLK, (n + 1) * BLK)
        total = part_ref[0, span, :].astype(jnp.float32)
        for q in range(1, part_ref.shape[0]):
            total = total + part_ref[q, span, :].astype(jnp.float32)
        before = jnp.broadcast_to(accum_ref[n : n + 1, :], (BLK, BLK)).T
        accum = before + jnp.mean(total * total, axis=1, keepdims=True)
        out_ref[n : n + 1, :] = accum.T[0:1, :]
        step_size = learn_rate / (jnp.sqrt(accum) + ada_epsilon)
        rows = (row_ref[span, :].astype(jnp.float32) - step_size * total).astype(jnp.bfloat16)
        for q in range(copies_ref.shape[0]):
            copies_ref[q, span, :] = rows


def update(received, rows, accum):
    return pl.pallas_call(
        update_body,
        in_specs=[VMEM, VMEM, VMEM],
        out_specs=[VMEM, VMEM],
        out_shape=[
            jax.ShapeDtypeStruct(received.shape, jnp.bfloat16),
            jax.ShapeDtypeStruct(accum.shape, jnp.float32),
        ],
        name="update",
    )(received, rows, accum)


def swap(blocks, axis):
    return lax.all_to_all(blocks, axis, split_axis=0, concat_axis=0, tiled=True)


def shards(
    own_table,
    own_accum,
    sectioned_rows,
    sectioned_accum,
    fold_pairs,
    slab_ids,
    bag_blocks,
    bag_counts,
    bag_weights,
    top_weight,
    hidden_grad,
):
    tables = lax.axis_size("table")
    parts = lax.axis_size("dp")
    share = NB * BLK // parts
    bag_total = bag_blocks.shape[0]
    copies, order, accum = pick(fold_pairs, slab_ids, sectioned_rows, sectioned_accum, own_accum, parts)
    slab_rows = swap(copies, "dp").reshape(SLAB * BLK, E)
    blocks = bag_blocks[:, 0, :].T
    counts = bag_counts.reshape(1, bag_total)
    weights = bag_weights.reshape(bag_total * K, BLK)
    before = early(blocks, counts, weights, bag_total // (2 * BLK))
    pooled, before, after, rows = pool(order, blocks, counts, own_table, slab_rows, weights, before, share)
    fan = swap(pooled.reshape(tables, bag_total // tables, E), "table")
    hidden, back = layer(fan, top_weight, hidden_grad)
    row_grad = grad(before, after, swap(back, "table").reshape(bag_total, E))
    received = swap(row_grad.reshape(parts, share, E), "dp")
    copies, accum = update(received, rows, accum)
    new_table = swap(copies, "dp").reshape(NB * BLK, E)
    return (new_table, accum.reshape(share), hidden)


def solution(mesh):
    placed = (
        P("table", None),
        P("table"),
        P(None, "dp", None),
        P(),
        P(),
        P(),
        P("dp", "table", None),
        P("dp", "table"),
        P("dp", "table", None, None),
        P(),
        P(("dp", "table"), None),
    )
    return jax.shard_map(
        shards,
        mesh=mesh,
        in_specs=placed,
        out_specs=(P("table", None), P(("table", "dp")), P(("dp", "table"), None)),
        check_vma=False,
    )
```

```python
import functools

import jax
import jax.numpy as jnp
from jax import lax
from jax.experimental import pallas as pl
from jax.experimental.pallas import tpu as pltpu
from jax.sharding import PartitionSpec as P

E = 128
BLK = 128
R = 10
SLAB = 6
K = 4
NB = R + SLAB
TILE = 16
EACH = 4
WIDE = K * BLK

learn_rate = 0.5
ada_epsilon = 1e-08

ANY = pl.BlockSpec(memory_space=pl.ANY)
HBM = pl.BlockSpec(memory_space=pltpu.HBM)
SMEM = pl.BlockSpec(memory_space=pltpu.SMEM)
VMEM = pl.BlockSpec(memory_space=pltpu.VMEM)


def fill_perm(perm_ref):
    row = lax.broadcasted_iota(jnp.int32, (WIDE, BLK), 0)
    lane = lax.broadcasted_iota(jnp.int32, (WIDE, BLK), 1)
    for k in range(K):
        perm_ref[k] = jnp.where(row == lane * K + k, 1.0, 0.0).astype(jnp.bfloat16)


def turn(window, at, perm_ref, part_ref, group):
    turned = jnp.concatenate([window[pl.ds(at + BLK * n, BLK), :].T for n in range(K)], axis=1)
    for k in range(0, K, 2):
        right = jnp.concatenate([perm_ref[k], perm_ref[k + 1]], axis=1)
        got = jnp.dot(turned, right, preferred_element_type=jnp.float32).astype(jnp.bfloat16)
        part_ref[group, k] = got[:, :BLK]
        part_ref[group, k + 1] = got[:, BLK:]


def place(block_ref, count_ref, base, part_ref, group, out_ref, at):
    blocks = block_ref[:, pl.ds(base, BLK)]
    counts = count_ref[:, pl.ds(base, BLK)]
    names = []
    for k in range(K):
        name = jnp.where(counts > k, blocks[k : k + 1, :], NB).astype(jnp.float32)
        names.append(jnp.broadcast_to(name, (TILE, BLK)).astype(jnp.bfloat16))
    for m in range(NB):
        hits = [names[k] == jnp.bfloat16(m) for k in range(K)]
        for s in range(0, BLK, TILE):
            value = jnp.zeros((TILE, BLK), jnp.bfloat16)
            for k in range(K):
                value = jnp.where(hits[k], part_ref[group, k, s : s + TILE, :], value)
            out_ref[at, m * BLK + s : m * BLK + s + TILE, :] = value


def fetches(source, base, target, sem, pieces):
    size = target.shape[0] // pieces

    def piece(n):
        return pltpu.make_async_copy(
            source.at[pl.ds(base + n * size, size)], target.at[pl.ds(n * size, size)], sem.at[n]
        )

    return piece


def early_body(weight_hbm, out_hbm, window, perm_ref, part_ref, in_sem, out_sem):
    groups = part_ref.shape[0]
    pieces = groups // EACH
    fetch = fetches(weight_hbm, 0, window, in_sem, pieces)

    def send(piece):
        span = pl.ds(pl.multiple_of(piece * EACH, EACH), EACH)
        return pltpu.make_async_copy(part_ref.at[span], out_hbm.at[span], out_sem.at[piece])

    for n in range(pieces):
        fetch(n).start()
    fill_perm(perm_ref)

    def step(piece, carry):
        fetch(piece).wait()
        for g in range(EACH):
            group = piece * EACH + g
            turn(window, pl.multiple_of(group * WIDE, WIDE), perm_ref, part_ref, group)
        send(piece).start()
        return carry

    lax.fori_loop(0, pieces, step, 0)
    for n in range(pieces):
        send(n).wait()


def early(weights):
    groups = weights.shape[0] // WIDE
    parts = (groups, K, BLK, BLK)
    sem = pltpu.SemaphoreType.DMA((groups // EACH,))
    return pl.pallas_call(
        early_body,
        in_specs=[HBM],
        out_specs=ANY,
        out_shape=jax.ShapeDtypeStruct(parts, jnp.bfloat16),
        scratch_shapes=[
            pltpu.VMEM(weights.shape, jnp.bfloat16),
            pltpu.VMEM((K, WIDE, BLK), jnp.bfloat16),
            pltpu.VMEM(parts, jnp.bfloat16),
            sem,
            sem,
        ],
        cost_estimate=pl.CostEstimate(
            flops=2 * weights.size * WIDE * 4, bytes_accessed=weights.size * 4, transcendentals=0
        ),
        name="early",
    )(weights)


def pool_body(
    order_ref, block_ref, count_ref, own_ref, slab_ref, part_hbm,
    out_hbm, first, second, share_ref,
    part_ref, table_ref, turned_ref, pooled, part_sem, pool_sem,
):
    half = first.shape[0]
    pieces = 2 * half // EACH
    fetch = fetches(part_hbm, 0, part_ref, part_sem, pieces)
    for n in range(pieces):
        fetch(n).start()
    table_ref[0 : R * BLK, :] = own_ref[...]
    for j in range(SLAB):
        at = pl.multiple_of(order_ref[j] * BLK, BLK)
        table_ref[(R + j) * BLK : (R + j + 1) * BLK, :] = slab_ref[pl.ds(at, BLK), :]
    for m in range(NB):
        turned_ref[:, m * BLK : (m + 1) * BLK] = table_ref[m * BLK : (m + 1) * BLK, :].T
    share = share_ref.shape[0]
    share_ref[...] = table_ref[pl.ds(pl.multiple_of(lax.axis_index("dp") * share, share), share), :]

    def send(start, count):
        span = pl.ds(start * BLK, count * BLK)
        return pltpu.make_async_copy(pooled.at[span, :], out_hbm.at[span, :], pool_sem)

    def sums(source, at, count, to):
        right = jnp.concatenate([source[at + q] for q in range(count)], axis=1)
        got = jnp.dot(turned_ref[...], right, preferred_element_type=jnp.float32)
        pooled[pl.ds(pl.multiple_of(to * BLK, BLK), count * BLK), :] = got.T.astype(jnp.bfloat16)

    def put(group, target, at):
        place(block_ref, count_ref, pl.multiple_of(group * BLK, BLK), part_ref, group, target, at)

    def fill(pair, carry):
        @pl.when(lax.rem(pair, EACH // 2) == 0)
        def _():
            fetch(pair // (EACH // 2)).wait()

        for g in range(2):
            put(2 * pair + g, first, 2 * pair + g)
        return carry

    lax.fori_loop(0, half // 2, fill, 0)

    def both(pair, carry):
        @pl.when(lax.rem(pair, EACH // 2) == 0)
        def _():
            fetch(half // EACH + pair // (EACH // 2)).wait()

        for g in range(2):
            put(half + 2 * pair + g, second, 2 * pair + g)
        sums(first, 2 * pair, 2, 2 * pair)
        return carry

    lax.fori_loop(0, half // 2, both, 0)
    send(0, half).start()

    def rest(n, carry):
        sums(second, 4 * n, 4, half + 4 * n)
        return carry

    lax.fori_loop(0, half // 4, rest, 0)
    send(half, half).start()
    send(0, 2 * half).wait()


def pool(order, blocks, counts, own, slab, parts, share):
    bags = blocks.shape[1]
    matrix = pltpu.VMEM((bags // (2 * BLK), NB * BLK, BLK), jnp.bfloat16)
    return pl.pallas_call(
        pool_body,
        in_specs=[SMEM, VMEM, VMEM, VMEM, VMEM, HBM],
        out_specs=[ANY, VMEM, VMEM, VMEM],
        out_shape=[
            jax.ShapeDtypeStruct((bags, E), jnp.bfloat16),
            matrix,
            matrix,
            jax.ShapeDtypeStruct((share, E), jnp.bfloat16),
        ],
        scratch_shapes=[
            pltpu.VMEM(parts.shape, jnp.bfloat16),
            pltpu.VMEM((NB * BLK, E), jnp.bfloat16),
            pltpu.VMEM((E, NB * BLK), jnp.bfloat16),
            pltpu.VMEM((bags, E), jnp.bfloat16),
            pltpu.SemaphoreType.DMA((parts.shape[0] // EACH,)),
            pltpu.SemaphoreType.DMA,
        ],
        cost_estimate=pl.CostEstimate(
            flops=2 * bags * NB * BLK * E, bytes_accessed=bags * NB * BLK * 2, transcendentals=0
        ),
        compiler_params=pltpu.CompilerParams(vmem_limit_bytes=40 << 20),
        name="pool",
    )(order, blocks, counts, own, slab, parts)


def layer_body(pair, fan_ref, top_ref, cot_ref, hid_hbm, out_ref, hid_ref, sum_ref, pre_ref, sem):
    fan, rows, _ = fan_ref.shape
    wide = pair * E
    steps = fan // pair
    send_hid = pltpu.make_async_copy(hid_ref, hid_hbm, sem)
    for p in range(steps):
        left = jnp.concatenate([fan_ref[p * pair + q] for q in range(pair)], axis=1)
        part = jnp.dot(left, top_ref[p * wide : (p + 1) * wide, :], preferred_element_type=jnp.float32)
        if p == 0:
            sum_ref[...] = part
        else:
            sum_ref[...] += part
    preact = sum_ref[...]
    gate = jax.nn.sigmoid(preact)
    hid_ref[...] = (preact * gate).astype(jnp.bfloat16)
    send_hid.start()
    slope = gate * (1.0 + preact * (1.0 - gate))
    pre_ref[...] = (cot_ref[...].astype(jnp.float32) * slope).astype(jnp.bfloat16)
    for p in range(steps):
        back = lax.dot_general(
            pre_ref[...],
            top_ref[p * wide : (p + 1) * wide, :],
            (((1,), (1,)), ((), ())),
            preferred_element_type=jnp.float32,
        ).astype(jnp.bfloat16)
        for q in range(pair):
            out_ref[p * pair + q] = back[:, q * E : (q + 1) * E]
    send_hid.wait()


def layer(fan, top_weight, cotangent, pair=4):
    tables, rows, _ = fan.shape
    hidden = top_weight.shape[1]
    return pl.pallas_call(
        functools.partial(layer_body, pair),
        in_specs=[VMEM, VMEM, VMEM],
        out_specs=[HBM, VMEM],
        out_shape=[
            jax.ShapeDtypeStruct((rows, hidden), jnp.bfloat16),
            jax.ShapeDtypeStruct((tables, rows, E), jnp.bfloat16),
        ],
        scratch_shapes=[
            pltpu.VMEM((rows, hidden), jnp.bfloat16),
            pltpu.VMEM((rows, hidden), jnp.float32),
            pltpu.VMEM((rows, hidden), jnp.bfloat16),
            pltpu.SemaphoreType.DMA,
        ],
        cost_estimate=pl.CostEstimate(
            flops=4 * rows * top_weight.size, bytes_accessed=rows * hidden * 6, transcendentals=rows * hidden
        ),
        compiler_params=pltpu.CompilerParams(vmem_limit_bytes=16 << 20),
        name="layer",
    )(fan, top_weight, cotangent)


def grad_body(tile, before, after, grad_ref, out_hbm, out_ref, sem):
    def send(n):
        span = pl.ds(pl.multiple_of(n * tile, tile), tile)
        return pltpu.make_async_copy(out_ref.at[span, :], out_hbm.at[span, :], sem)

    def rows(n, carry):
        span = pl.ds(pl.multiple_of(n * tile, tile), tile)
        left = [ref[q, span, :] for ref in (before, after) for q in range(ref.shape[0])]
        total = jnp.dot(jnp.concatenate(left, axis=1), grad_ref[...], preferred_element_type=jnp.float32)
        out_ref[span, :] = total.astype(jnp.bfloat16)
        send(n).start()
        return carry

    lax.fori_loop(0, NB * BLK // tile, rows, 0)
    pltpu.make_async_copy(out_ref, out_hbm, sem).wait()


def grad(before, after, pooled_grad, tile=512):
    return pl.pallas_call(
        functools.partial(grad_body, tile),
        in_specs=[VMEM, VMEM, VMEM],
        out_specs=ANY,
        out_shape=jax.ShapeDtypeStruct((NB * BLK, E), jnp.bfloat16),
        scratch_shapes=[pltpu.VMEM((NB * BLK, E), jnp.bfloat16), pltpu.SemaphoreType.DMA],
        cost_estimate=pl.CostEstimate(
            flops=2 * pooled_grad.size * NB * BLK, bytes_accessed=pooled_grad.size * 4, transcendentals=0
        ),
        compiler_params=pltpu.CompilerParams(vmem_limit_bytes=8 << 20),
        name="grad",
    )(before, after, pooled_grad)


def pick_body(pair_ref, ids_ref, sect_ref, state_ref, accum_ref, copies_ref, order_ref, out_ref):
    partner = pair_ref[lax.axis_index("table")]
    for n in range(copies_ref.shape[0]):
        copies_ref[n] = sect_ref[partner]
    for j in range(SLAB):
        order_ref[j] = ids_ref[j, partner]
    count = out_ref.shape[0]
    for n in range(count):
        block = lax.axis_index("dp") * count + n
        own = accum_ref[pl.ds(jnp.minimum(block, R - 1), 1), :]
        fold = pl.multiple_of(ids_ref[jnp.maximum(block - R, 0), partner] * BLK, BLK)
        states = state_ref[:, pl.ds(fold, BLK)]
        mine = lax.broadcasted_iota(jnp.int32, states.shape, 0) == partner
        other = jnp.sum(jnp.where(mine, states, 0.0), axis=0, keepdims=True)
        out_ref[n : n + 1, :] = jnp.where(block < R, own, other)


def pick(fold_pairs, slab_ids, sectioned_rows, sectioned_accum, own_accum, parts):
    _, size, width = sectioned_rows.shape
    return pl.pallas_call(
        pick_body,
        in_specs=[SMEM, SMEM, VMEM, VMEM, VMEM],
        out_specs=[VMEM, SMEM, VMEM],
        out_shape=[
            jax.ShapeDtypeStruct((parts, size, width), jnp.bfloat16),
            jax.ShapeDtypeStruct((SLAB,), jnp.int32),
            jax.ShapeDtypeStruct((NB // parts, BLK), jnp.float32),
        ],
        name="pick",
    )(fold_pairs, slab_ids.T, sectioned_rows, sectioned_accum, own_accum.reshape(R, BLK))


def update_body(part_ref, row_ref, accum_ref, copies_ref, out_ref):
    for n in range(accum_ref.shape[0]):
        span = slice(n * BLK, (n + 1) * BLK)
        total = part_ref[0, span, :].astype(jnp.float32)
        for q in range(1, part_ref.shape[0]):
            total = total + part_ref[q, span, :].astype(jnp.float32)
        before = jnp.broadcast_to(accum_ref[n : n + 1, :], (BLK, BLK)).T
        accum = before + jnp.mean(total * total, axis=1, keepdims=True)
        out_ref[n : n + 1, :] = accum.T[0:1, :]
        step_size = learn_rate / (jnp.sqrt(accum) + ada_epsilon)
        rows = (row_ref[span, :].astype(jnp.float32) - step_size * total).astype(jnp.bfloat16)
        for q in range(copies_ref.shape[0]):
            copies_ref[q, span, :] = rows


def update(received, rows, accum):
    return pl.pallas_call(
        update_body,
        in_specs=[VMEM, VMEM, VMEM],
        out_specs=[VMEM, VMEM],
        out_shape=[
            jax.ShapeDtypeStruct(received.shape, jnp.bfloat16),
            jax.ShapeDtypeStruct(accum.shape, jnp.float32),
        ],
        name="update",
    )(received, rows, accum)


def swap(blocks, axis):
    return lax.all_to_all(blocks, axis, split_axis=0, concat_axis=0, tiled=True)


def shards(
    own_table,
    own_accum,
    sectioned_rows,
    sectioned_accum,
    fold_pairs,
    slab_ids,
    bag_blocks,
    bag_counts,
    bag_weights,
    top_weight,
    hidden_grad,
):
    tables = lax.axis_size("table")
    parts = lax.axis_size("dp")
    share = NB * BLK // parts
    bag_total = bag_blocks.shape[0]
    copies, order, accum = pick(fold_pairs, slab_ids, sectioned_rows, sectioned_accum, own_accum, parts)
    slab_rows = swap(copies, "dp").reshape(SLAB * BLK, E)
    blocks = bag_blocks[:, 0, :].T
    counts = bag_counts.reshape(1, bag_total)
    weights = bag_weights.reshape(bag_total * K, BLK)
    parts_turned = early(weights)
    pooled, before, after, rows = pool(order, blocks, counts, own_table, slab_rows, parts_turned, share)
    fan = swap(pooled.reshape(tables, bag_total // tables, E), "table")
    hidden, back = layer(fan, top_weight, hidden_grad)
    row_grad = grad(before, after, swap(back, "table").reshape(bag_total, E))
    received = swap(row_grad.reshape(parts, share, E), "dp")
    copies, accum = update(received, rows, accum)
    new_table = swap(copies, "dp").reshape(NB * BLK, E)
    return (new_table, accum.reshape(share), hidden)


def solution(mesh):
    placed = (
        P("table", None),
        P("table"),
        P(None, "dp", None),
        P(),
        P(),
        P(),
        P("dp", "table", None),
        P("dp", "table"),
        P("dp", "table", None, None),
        P(),
        P(("dp", "table"), None),
    )
    return jax.shard_map(
        shards,
        mesh=mesh,
        in_specs=placed,
        out_specs=(P("table", None), P(("table", "dp")), P(("dp", "table"), None)),
        check_vma=False,
    )
```

```python
import functools

import jax
import jax.numpy as jnp
from jax import lax
from jax.experimental import pallas as pl
from jax.experimental.pallas import tpu as pltpu
from jax.sharding import PartitionSpec as P

E = 128
BLK = 128
R = 10
SLAB = 6
K = 4
NB = R + SLAB
TILE = 16
EACH = 4
WIDE = K * BLK

learn_rate = 0.5
ada_epsilon = 1e-08

ANY = pl.BlockSpec(memory_space=pl.ANY)
HBM = pl.BlockSpec(memory_space=pltpu.HBM)
SMEM = pl.BlockSpec(memory_space=pltpu.SMEM)
VMEM = pl.BlockSpec(memory_space=pltpu.VMEM)


def fill_perm(perm_ref):
    row = lax.broadcasted_iota(jnp.int32, (WIDE, BLK), 0)
    lane = lax.broadcasted_iota(jnp.int32, (WIDE, BLK), 1)
    for k in range(K):
        perm_ref[k] = jnp.where(row == lane * K + k, 1.0, 0.0).astype(jnp.bfloat16)


def turn(window, at, perm_ref, part_ref, group):
    turned = jnp.concatenate([window[pl.ds(at + BLK * n, BLK), :].T for n in range(K)], axis=1)
    for k in range(0, K, 2):
        right = jnp.concatenate([perm_ref[k], perm_ref[k + 1]], axis=1)
        got = jnp.dot(turned, right, preferred_element_type=jnp.float32).astype(jnp.bfloat16)
        part_ref[group, k] = got[:, :BLK]
        part_ref[group, k + 1] = got[:, BLK:]


def place(block_ref, count_ref, base, part_ref, group, out_ref, at):
    blocks = block_ref[:, pl.ds(base, BLK)]
    counts = count_ref[:, pl.ds(base, BLK)]
    names = []
    for k in range(K):
        name = jnp.where(counts > k, blocks[k : k + 1, :], NB).astype(jnp.float32)
        names.append(jnp.broadcast_to(name, (TILE, BLK)).astype(jnp.bfloat16))
    for m in range(NB):
        hits = [names[k] == jnp.bfloat16(m) for k in range(K)]
        for s in range(0, BLK, TILE):
            value = jnp.zeros((TILE, BLK), jnp.bfloat16)
            for k in range(K):
                value = jnp.where(hits[k], part_ref[group, k, s : s + TILE, :], value)
            out_ref[at, m * BLK + s : m * BLK + s + TILE, :] = value


def fetches(source, base, target, sem, pieces):
    size = target.shape[0] // pieces

    def piece(n):
        return pltpu.make_async_copy(
            source.at[pl.ds(base + n * size, size)], target.at[pl.ds(n * size, size)], sem.at[n]
        )

    return piece


def early_body(weight_hbm, out_hbm, window, perm_ref, part_ref, in_sem, out_sem):
    groups = part_ref.shape[0]
    pieces = groups // EACH
    fetch = fetches(weight_hbm, 0, window, in_sem, pieces)

    def send(piece):
        span = pl.ds(pl.multiple_of(piece * EACH, EACH), EACH)
        return pltpu.make_async_copy(part_ref.at[span], out_hbm.at[span], out_sem.at[piece])

    for n in range(pieces):
        fetch(n).start()
    fill_perm(perm_ref)

    def step(piece, carry):
        fetch(piece).wait()
        for g in range(EACH):
            group = piece * EACH + g
            turn(window, pl.multiple_of(group * WIDE, WIDE), perm_ref, part_ref, group)
        send(piece).start()
        return carry

    lax.fori_loop(0, pieces, step, 0)
    for n in range(pieces):
        send(n).wait()


def early(weights):
    groups = weights.shape[0] // WIDE
    parts = (groups, K, BLK, BLK)
    sem = pltpu.SemaphoreType.DMA((groups // EACH,))
    return pl.pallas_call(
        early_body,
        in_specs=[HBM],
        out_specs=ANY,
        out_shape=jax.ShapeDtypeStruct(parts, jnp.bfloat16),
        scratch_shapes=[
            pltpu.VMEM(weights.shape, jnp.bfloat16),
            pltpu.VMEM((K, WIDE, BLK), jnp.bfloat16),
            pltpu.VMEM(parts, jnp.bfloat16),
            sem,
            sem,
        ],
        cost_estimate=pl.CostEstimate(
            flops=2 * weights.size * WIDE * 4, bytes_accessed=weights.size * 4, transcendentals=0
        ),
        name="early",
    )(weights)


def pool_body(
    order_ref, block_ref, count_ref, own_ref, slab_hbm, part_hbm,
    out_hbm, first, second, share_ref,
    part_ref, table_ref, turned_ref, pooled, slab_ref, part_sem, pool_sem,
):
    half = first.shape[0]
    pieces = 2 * half // EACH
    fetch = fetches(part_hbm, 0, part_ref, part_sem, pieces)
    slab_copy = pltpu.make_async_copy(slab_hbm, slab_ref, pool_sem)
    slab_copy.start()
    for n in range(pieces):
        fetch(n).start()
    table_ref[0 : R * BLK, :] = own_ref[...]
    slab_copy.wait()
    for j in range(SLAB):
        at = pl.multiple_of(order_ref[j] * BLK, BLK)
        table_ref[(R + j) * BLK : (R + j + 1) * BLK, :] = slab_ref[pl.ds(at, BLK), :]
    for m in range(NB):
        turned_ref[:, m * BLK : (m + 1) * BLK] = table_ref[m * BLK : (m + 1) * BLK, :].T
    share = share_ref.shape[0]
    share_ref[...] = table_ref[pl.ds(pl.multiple_of(lax.axis_index("dp") * share, share), share), :]

    def send(start, count):
        span = pl.ds(start * BLK, count * BLK)
        return pltpu.make_async_copy(pooled.at[span, :], out_hbm.at[span, :], pool_sem)

    def sums(source, at, count, to):
        right = jnp.concatenate([source[at + q] for q in range(count)], axis=1)
        got = jnp.dot(turned_ref[...], right, preferred_element_type=jnp.float32)
        pooled[pl.ds(pl.multiple_of(to * BLK, BLK), count * BLK), :] = got.T.astype(jnp.bfloat16)

    def put(group, target, at):
        place(block_ref, count_ref, pl.multiple_of(group * BLK, BLK), part_ref, group, target, at)

    def fill(pair, carry):
        @pl.when(lax.rem(pair, EACH // 2) == 0)
        def _():
            fetch(pair // (EACH // 2)).wait()

        for g in range(2):
            put(2 * pair + g, first, 2 * pair + g)
        return carry

    lax.fori_loop(0, half // 2, fill, 0)

    def both(pair, carry):
        @pl.when(lax.rem(pair, EACH // 2) == 0)
        def _():
            fetch(half // EACH + pair // (EACH // 2)).wait()

        for g in range(2):
            put(half + 2 * pair + g, second, 2 * pair + g)
        sums(first, 2 * pair, 2, 2 * pair)
        return carry

    lax.fori_loop(0, half // 2, both, 0)
    send(0, half).start()

    def rest(n, carry):
        sums(second, 4 * n, 4, half + 4 * n)
        return carry

    lax.fori_loop(0, half // 4, rest, 0)
    send(half, half).start()
    send(0, 2 * half).wait()


def pool(order, blocks, counts, own, slab, parts, share):
    bags = blocks.shape[1]
    matrix = pltpu.VMEM((bags // (2 * BLK), NB * BLK, BLK), jnp.bfloat16)
    return pl.pallas_call(
        pool_body,
        in_specs=[SMEM, VMEM, VMEM, VMEM, ANY, HBM],
        out_specs=[ANY, VMEM, VMEM, VMEM],
        out_shape=[
            jax.ShapeDtypeStruct((bags, E), jnp.bfloat16),
            matrix,
            matrix,
            jax.ShapeDtypeStruct((share, E), jnp.bfloat16),
        ],
        scratch_shapes=[
            pltpu.VMEM(parts.shape, jnp.bfloat16),
            pltpu.VMEM((NB * BLK, E), jnp.bfloat16),
            pltpu.VMEM((E, NB * BLK), jnp.bfloat16),
            pltpu.VMEM((bags, E), jnp.bfloat16),
            pltpu.VMEM(slab.shape, jnp.bfloat16),
            pltpu.SemaphoreType.DMA((parts.shape[0] // EACH,)),
            pltpu.SemaphoreType.DMA,
        ],
        cost_estimate=pl.CostEstimate(
            flops=2 * bags * NB * BLK * E, bytes_accessed=bags * NB * BLK * 2, transcendentals=0
        ),
        compiler_params=pltpu.CompilerParams(vmem_limit_bytes=36 << 20),
        name="pool",
    )(order, blocks, counts, own, slab, parts)


def layer_body(pair, fan_ref, top_ref, cot_ref, hid_hbm, out_ref, hid_ref, sum_ref, pre_ref, sem):
    fan, rows, _ = fan_ref.shape
    wide = pair * E
    steps = fan // pair
    send_hid = pltpu.make_async_copy(hid_ref, hid_hbm, sem)
    for p in range(steps):
        left = jnp.concatenate([fan_ref[p * pair + q] for q in range(pair)], axis=1)
        part = jnp.dot(left, top_ref[p * wide : (p + 1) * wide, :], preferred_element_type=jnp.float32)
        if p == 0:
            sum_ref[...] = part
        else:
            sum_ref[...] += part
    preact = sum_ref[...]
    gate = jax.nn.sigmoid(preact)
    hid_ref[...] = (preact * gate).astype(jnp.bfloat16)
    send_hid.start()
    slope = gate * (1.0 + preact * (1.0 - gate))
    pre_ref[...] = (cot_ref[...].astype(jnp.float32) * slope).astype(jnp.bfloat16)
    for p in range(steps):
        back = lax.dot_general(
            pre_ref[...],
            top_ref[p * wide : (p + 1) * wide, :],
            (((1,), (1,)), ((), ())),
            preferred_element_type=jnp.float32,
        ).astype(jnp.bfloat16)
        for q in range(pair):
            out_ref[p * pair + q] = back[:, q * E : (q + 1) * E]
    send_hid.wait()


def layer(fan, top_weight, cotangent, pair=4):
    tables, rows, _ = fan.shape
    hidden = top_weight.shape[1]
    return pl.pallas_call(
        functools.partial(layer_body, pair),
        in_specs=[VMEM, VMEM, VMEM],
        out_specs=[HBM, VMEM],
        out_shape=[
            jax.ShapeDtypeStruct((rows, hidden), jnp.bfloat16),
            jax.ShapeDtypeStruct((tables, rows, E), jnp.bfloat16),
        ],
        scratch_shapes=[
            pltpu.VMEM((rows, hidden), jnp.bfloat16),
            pltpu.VMEM((rows, hidden), jnp.float32),
            pltpu.VMEM((rows, hidden), jnp.bfloat16),
            pltpu.SemaphoreType.DMA,
        ],
        cost_estimate=pl.CostEstimate(
            flops=4 * rows * top_weight.size, bytes_accessed=rows * hidden * 6, transcendentals=rows * hidden
        ),
        compiler_params=pltpu.CompilerParams(vmem_limit_bytes=16 << 20),
        name="layer",
    )(fan, top_weight, cotangent)


def grad_body(tile, before, after, grad_ref, out_hbm, out_ref, sem):
    def send(n):
        span = pl.ds(pl.multiple_of(n * tile, tile), tile)
        return pltpu.make_async_copy(out_ref.at[span, :], out_hbm.at[span, :], sem)

    def rows(n, carry):
        span = pl.ds(pl.multiple_of(n * tile, tile), tile)
        left = [ref[q, span, :] for ref in (before, after) for q in range(ref.shape[0])]
        total = jnp.dot(jnp.concatenate(left, axis=1), grad_ref[...], preferred_element_type=jnp.float32)
        out_ref[span, :] = total.astype(jnp.bfloat16)
        send(n).start()
        return carry

    lax.fori_loop(0, NB * BLK // tile, rows, 0)
    pltpu.make_async_copy(out_ref, out_hbm, sem).wait()


def grad(before, after, pooled_grad, tile=512):
    return pl.pallas_call(
        functools.partial(grad_body, tile),
        in_specs=[VMEM, VMEM, VMEM],
        out_specs=ANY,
        out_shape=jax.ShapeDtypeStruct((NB * BLK, E), jnp.bfloat16),
        scratch_shapes=[pltpu.VMEM((NB * BLK, E), jnp.bfloat16), pltpu.SemaphoreType.DMA],
        cost_estimate=pl.CostEstimate(
            flops=2 * pooled_grad.size * NB * BLK, bytes_accessed=pooled_grad.size * 4, transcendentals=0
        ),
        compiler_params=pltpu.CompilerParams(vmem_limit_bytes=8 << 20),
        name="grad",
    )(before, after, pooled_grad)


def pick_body(pair_ref, ids_ref, sect_hbm, state_ref, accum_ref, copies_ref, order_ref, out_ref, sem):
    partner = pair_ref[lax.axis_index("table")]
    copies = [pltpu.make_async_copy(sect_hbm.at[partner], copies_ref.at[n], sem.at[n]) for n in range(copies_ref.shape[0])]
    for copy in copies:
        copy.start()
    for j in range(SLAB):
        order_ref[j] = ids_ref[j, partner]
    count = out_ref.shape[0]
    for n in range(count):
        block = lax.axis_index("dp") * count + n
        own = accum_ref[pl.ds(jnp.minimum(block, R - 1), 1), :]
        fold = pl.multiple_of(ids_ref[jnp.maximum(block - R, 0), partner] * BLK, BLK)
        states = state_ref[:, pl.ds(fold, BLK)]
        mine = lax.broadcasted_iota(jnp.int32, states.shape, 0) == partner
        other = jnp.sum(jnp.where(mine, states, 0.0), axis=0, keepdims=True)
        out_ref[n : n + 1, :] = jnp.where(block < R, own, other)
    for copy in copies:
        copy.wait()


def pick(fold_pairs, slab_ids, sectioned_rows, sectioned_accum, own_accum, parts):
    _, size, width = sectioned_rows.shape
    return pl.pallas_call(
        pick_body,
        in_specs=[SMEM, SMEM, HBM, VMEM, VMEM],
        out_specs=[VMEM, SMEM, VMEM],
        out_shape=[
            jax.ShapeDtypeStruct((parts, size, width), jnp.bfloat16),
            jax.ShapeDtypeStruct((SLAB,), jnp.int32),
            jax.ShapeDtypeStruct((NB // parts, BLK), jnp.float32),
        ],
        scratch_shapes=[pltpu.SemaphoreType.DMA((parts,))],
        name="pick",
    )(fold_pairs, slab_ids.T, sectioned_rows, sectioned_accum, own_accum.reshape(R, BLK))


def update_body(part_ref, row_ref, accum_ref, new_ref, out_ref):
    for n in range(accum_ref.shape[0]):
        span = slice(n * BLK, (n + 1) * BLK)
        total = part_ref[0, span, :].astype(jnp.float32)
        for q in range(1, part_ref.shape[0]):
            total = total + part_ref[q, span, :].astype(jnp.float32)
        before = jnp.broadcast_to(accum_ref[n : n + 1, :], (BLK, BLK)).T
        accum = before + jnp.mean(total * total, axis=1, keepdims=True)
        out_ref[n : n + 1, :] = accum.T[0:1, :]
        step_size = learn_rate / (jnp.sqrt(accum) + ada_epsilon)
        new_ref[span, :] = (row_ref[span, :].astype(jnp.float32) - step_size * total).astype(jnp.bfloat16)


def update(received, rows, accum):
    return pl.pallas_call(
        update_body,
        in_specs=[VMEM, VMEM, VMEM],
        out_specs=[VMEM, VMEM],
        out_shape=[
            jax.ShapeDtypeStruct(rows.shape, jnp.bfloat16),
            jax.ShapeDtypeStruct(accum.shape, jnp.float32),
        ],
        compiler_params=pltpu.CompilerParams(vmem_limit_bytes=8 << 20),
        name="update",
    )(received, rows, accum)


def lay_body(near_ref, *refs):
    out_ref = refs[-1]
    size = near_ref.shape[0] // 2
    me = lax.axis_index("dp")
    across = out_ref.shape[0] // (2 * size)
    for step, ref in enumerate((near_ref,) + refs[:-1]):
        there = lax.rem(me // 2 + across - step, across) * 2
        for half, side in enumerate((lax.rem(me, 2), 1 - lax.rem(me, 2))):
            at = pl.multiple_of((there + side) * size, size)
            out_ref[pl.ds(at, size), :] = ref[half * size : (half + 1) * size, :]


def spread_rows(rows, parts):
    def along(block, step):
        return lax.ppermute(block, "dp", [(n, (n + 2 * step) % parts) for n in range(parts)])

    other = lax.ppermute(rows, "dp", [(n, n ^ 1) for n in range(parts)])
    near = jnp.concatenate([rows, other], axis=0)
    across = parts // 2
    order = [1, across - 1] + list(range(2, across - 1))
    far = dict((step, along(near, step)) for step in order)
    return pl.pallas_call(
        lay_body,
        in_specs=[VMEM] * across,
        out_specs=VMEM,
        out_shape=jax.ShapeDtypeStruct((parts * rows.shape[0], rows.shape[1]), rows.dtype),
        compiler_params=pltpu.CompilerParams(vmem_limit_bytes=8 << 20),
        name="lay",
    )(near, *[far[step] for step in range(1, across)])


def swap(blocks, axis):
    return lax.all_to_all(blocks, axis, split_axis=0, concat_axis=0, tiled=True)


def shards(
    own_table,
    own_accum,
    sectioned_rows,
    sectioned_accum,
    fold_pairs,
    slab_ids,
    bag_blocks,
    bag_counts,
    bag_weights,
    top_weight,
    hidden_grad,
):
    tables = lax.axis_size("table")
    parts = lax.axis_size("dp")
    share = NB * BLK // parts
    bag_total = bag_blocks.shape[0]
    copies, order, accum = pick(fold_pairs, slab_ids, sectioned_rows, sectioned_accum, own_accum, parts)
    slab_rows = swap(copies, "dp").reshape(SLAB * BLK, E)
    blocks = bag_blocks[:, 0, :].T
    counts = bag_counts.reshape(1, bag_total)
    weights = bag_weights.reshape(bag_total * K, BLK)
    parts_turned = early(weights)
    pooled, before, after, rows = pool(order, blocks, counts, own_table, slab_rows, parts_turned, share)
    fan = swap(pooled.reshape(tables, bag_total // tables, E), "table")
    hidden, back = layer(fan, top_weight, hidden_grad)
    row_grad = grad(before, after, swap(back, "table").reshape(bag_total, E))
    received = swap(row_grad.reshape(parts, share, E), "dp")
    new_rows, accum = update(received, rows, accum)
    new_table = spread_rows(new_rows, parts)
    return (new_table, accum.reshape(share), hidden)


def solution(mesh):
    placed = (
        P("table", None),
        P("table"),
        P(None, "dp", None),
        P(),
        P(),
        P(),
        P("dp", "table", None),
        P("dp", "table"),
        P("dp", "table", None, None),
        P(),
        P(("dp", "table"), None),
    )
    return jax.shard_map(
        shards,
        mesh=mesh,
        in_specs=placed,
        out_specs=(P("table", None), P(("table", "dp")), P(("dp", "table"), None)),
        check_vma=False,
    )
```

```python
import functools

import jax
import jax.numpy as jnp
from jax import lax
from jax.experimental import pallas as pl
from jax.experimental.pallas import tpu as pltpu
from jax.sharding import PartitionSpec as P

E = 128
BLK = 128
R = 10
SLAB = 6
K = 4
NB = R + SLAB
TILE = 16
EACH = 4
WIDE = K * BLK

learn_rate = 0.5
ada_epsilon = 1e-08

ANY = pl.BlockSpec(memory_space=pl.ANY)
HBM = pl.BlockSpec(memory_space=pltpu.HBM)
SMEM = pl.BlockSpec(memory_space=pltpu.SMEM)
VMEM = pl.BlockSpec(memory_space=pltpu.VMEM)


def fill_perm(perm_ref):
    row = lax.broadcasted_iota(jnp.int32, (WIDE, BLK), 0)
    lane = lax.broadcasted_iota(jnp.int32, (WIDE, BLK), 1)
    for k in range(K):
        perm_ref[k] = jnp.where(row == lane * K + k, 1.0, 0.0).astype(jnp.bfloat16)


def turn(window, at, perm_ref, part_ref, group):
    turned = jnp.concatenate([window[pl.ds(at + BLK * n, BLK), :].T for n in range(K)], axis=1)
    for k in range(0, K, 2):
        right = jnp.concatenate([perm_ref[k], perm_ref[k + 1]], axis=1)
        got = jnp.dot(turned, right, preferred_element_type=jnp.float32).astype(jnp.bfloat16)
        part_ref[group, k] = got[:, :BLK]
        part_ref[group, k + 1] = got[:, BLK:]


def place(block_ref, count_ref, base, part_ref, group, out_ref, at):
    blocks = block_ref[:, pl.ds(base, BLK)]
    counts = count_ref[:, pl.ds(base, BLK)]
    names = []
    for k in range(K):
        name = jnp.where(counts > k, blocks[k : k + 1, :], NB).astype(jnp.float32)
        names.append(jnp.broadcast_to(name, (TILE, BLK)).astype(jnp.bfloat16))
    for m in range(NB):
        hits = [names[k] == jnp.bfloat16(m) for k in range(K)]
        for s in range(0, BLK, TILE):
            value = jnp.zeros((TILE, BLK), jnp.bfloat16)
            for k in range(K):
                value = jnp.where(hits[k], part_ref[group, k, s : s + TILE, :], value)
            out_ref[at, m * BLK + s : m * BLK + s + TILE, :] = value


def fetches(source, base, target, sem, pieces):
    size = target.shape[0] // pieces

    def piece(n):
        return pltpu.make_async_copy(
            source.at[pl.ds(base + n * size, size)], target.at[pl.ds(n * size, size)], sem.at[n]
        )

    return piece


def early_body(weight_hbm, out_hbm, window, perm_ref, part_ref, in_sem, out_sem):
    groups = part_ref.shape[0]
    pieces = groups // EACH
    fetch = fetches(weight_hbm, 0, window, in_sem, pieces)

    def send(piece):
        span = pl.ds(pl.multiple_of(piece * EACH, EACH), EACH)
        return pltpu.make_async_copy(part_ref.at[span], out_hbm.at[span], out_sem.at[piece])

    for n in range(pieces):
        fetch(n).start()
    fill_perm(perm_ref)

    def step(piece, carry):
        fetch(piece).wait()
        for g in range(EACH):
            group = piece * EACH + g
            turn(window, pl.multiple_of(group * WIDE, WIDE), perm_ref, part_ref, group)
        send(piece).start()
        return carry

    lax.fori_loop(0, pieces, step, 0)
    for n in range(pieces):
        send(n).wait()


def early(weights):
    groups = weights.shape[0] // WIDE
    parts = (groups, K, BLK, BLK)
    sem = pltpu.SemaphoreType.DMA((groups // EACH,))
    return pl.pallas_call(
        early_body,
        in_specs=[HBM],
        out_specs=ANY,
        out_shape=jax.ShapeDtypeStruct(parts, jnp.bfloat16),
        scratch_shapes=[
            pltpu.VMEM(weights.shape, jnp.bfloat16),
            pltpu.VMEM((K, WIDE, BLK), jnp.bfloat16),
            pltpu.VMEM(parts, jnp.bfloat16),
            sem,
            sem,
        ],
        cost_estimate=pl.CostEstimate(
            flops=2 * weights.size * WIDE * 4, bytes_accessed=weights.size * 4, transcendentals=0
        ),
        name="early",
    )(weights)


def pool_body(
    order_ref, block_ref, count_ref, own_ref, slab_ref, part_hbm,
    pooled, first, second, share_ref,
    part_ref, table_ref, turned_ref, part_sem,
):
    half = first.shape[0]
    pieces = 2 * half // EACH
    fetch = fetches(part_hbm, 0, part_ref, part_sem, pieces)
    for n in range(pieces):
        fetch(n).start()
    table_ref[0 : R * BLK, :] = own_ref[...]
    for j in range(SLAB):
        at = pl.multiple_of(order_ref[j] * BLK, BLK)
        table_ref[(R + j) * BLK : (R + j + 1) * BLK, :] = slab_ref[pl.ds(at, BLK), :]
    for m in range(NB):
        turned_ref[:, m * BLK : (m + 1) * BLK] = table_ref[m * BLK : (m + 1) * BLK, :].T
    share = share_ref.shape[0]
    share_ref[...] = table_ref[pl.ds(pl.multiple_of(lax.axis_index("dp") * share, share), share), :]

    def sums(source, at, count, to):
        right = jnp.concatenate([source[at + q] for q in range(count)], axis=1)
        got = jnp.dot(turned_ref[...], right, preferred_element_type=jnp.float32)
        pooled[pl.ds(pl.multiple_of(to * BLK, BLK), count * BLK), :] = got.T.astype(jnp.bfloat16)

    def put(group, target, at):
        place(block_ref, count_ref, pl.multiple_of(group * BLK, BLK), part_ref, group, target, at)

    def fill(pair, carry):
        @pl.when(lax.rem(pair, EACH // 2) == 0)
        def _():
            fetch(pair // (EACH // 2)).wait()

        for g in range(2):
            put(2 * pair + g, first, 2 * pair + g)
        return carry

    lax.fori_loop(0, half // 2, fill, 0)

    def both(pair, carry):
        @pl.when(lax.rem(pair, EACH // 2) == 0)
        def _():
            fetch(half // EACH + pair // (EACH // 2)).wait()

        for g in range(2):
            put(half + 2 * pair + g, second, 2 * pair + g)
        sums(first, 2 * pair, 2, 2 * pair)
        return carry

    lax.fori_loop(0, half // 2, both, 0)

    def rest(n, carry):
        sums(second, 4 * n, 4, half + 4 * n)
        return carry

    lax.fori_loop(0, half // 4, rest, 0)


def pool(order, blocks, counts, own, slab, parts, share):
    bags = blocks.shape[1]
    matrix = pltpu.VMEM((bags // (2 * BLK), NB * BLK, BLK), jnp.bfloat16)
    return pl.pallas_call(
        pool_body,
        in_specs=[SMEM, VMEM, VMEM, VMEM, VMEM, HBM],
        out_specs=[VMEM, VMEM, VMEM, VMEM],
        out_shape=[
            jax.ShapeDtypeStruct((bags, E), jnp.bfloat16),
            matrix,
            matrix,
            jax.ShapeDtypeStruct((share, E), jnp.bfloat16),
        ],
        scratch_shapes=[
            pltpu.VMEM(parts.shape, jnp.bfloat16),
            pltpu.VMEM((NB * BLK, E), jnp.bfloat16),
            pltpu.VMEM((E, NB * BLK), jnp.bfloat16),
            pltpu.SemaphoreType.DMA((parts.shape[0] // EACH,)),
        ],
        cost_estimate=pl.CostEstimate(
            flops=2 * bags * NB * BLK * E, bytes_accessed=bags * NB * BLK * 2, transcendentals=0
        ),
        compiler_params=pltpu.CompilerParams(vmem_limit_bytes=36 << 20),
        name="pool",
    )(order, blocks, counts, own, slab, parts)


def layer_body(pair, fan_ref, top_ref, cot_ref, hid_hbm, out_ref, hid_ref, sum_ref, pre_ref, sem):
    fan, rows, _ = fan_ref.shape
    wide = pair * E
    steps = fan // pair
    send_hid = pltpu.make_async_copy(hid_ref, hid_hbm, sem)
    for p in range(steps):
        left = jnp.concatenate([fan_ref[p * pair + q] for q in range(pair)], axis=1)
        part = jnp.dot(left, top_ref[p * wide : (p + 1) * wide, :], preferred_element_type=jnp.float32)
        if p == 0:
            sum_ref[...] = part
        else:
            sum_ref[...] += part
    preact = sum_ref[...]
    gate = jax.nn.sigmoid(preact)
    hid_ref[...] = (preact * gate).astype(jnp.bfloat16)
    send_hid.start()
    slope = gate * (1.0 + preact * (1.0 - gate))
    pre_ref[...] = (cot_ref[...].astype(jnp.float32) * slope).astype(jnp.bfloat16)
    for p in range(steps):
        back = lax.dot_general(
            pre_ref[...],
            top_ref[p * wide : (p + 1) * wide, :],
            (((1,), (1,)), ((), ())),
            preferred_element_type=jnp.float32,
        ).astype(jnp.bfloat16)
        for q in range(pair):
            out_ref[p * pair + q] = back[:, q * E : (q + 1) * E]
    send_hid.wait()


def layer(fan, top_weight, cotangent, pair=4):
    tables, rows, _ = fan.shape
    hidden = top_weight.shape[1]
    return pl.pallas_call(
        functools.partial(layer_body, pair),
        in_specs=[VMEM, VMEM, VMEM],
        out_specs=[HBM, VMEM],
        out_shape=[
            jax.ShapeDtypeStruct((rows, hidden), jnp.bfloat16),
            jax.ShapeDtypeStruct((tables, rows, E), jnp.bfloat16),
        ],
        scratch_shapes=[
            pltpu.VMEM((rows, hidden), jnp.bfloat16),
            pltpu.VMEM((rows, hidden), jnp.float32),
            pltpu.VMEM((rows, hidden), jnp.bfloat16),
            pltpu.SemaphoreType.DMA,
        ],
        cost_estimate=pl.CostEstimate(
            flops=4 * rows * top_weight.size, bytes_accessed=rows * hidden * 6, transcendentals=rows * hidden
        ),
        compiler_params=pltpu.CompilerParams(vmem_limit_bytes=16 << 20),
        name="layer",
    )(fan, top_weight, cotangent)


def grad_body(tile, before, after, grad_ref, out_ref):
    def rows(n, carry):
        span = pl.ds(pl.multiple_of(n * tile, tile), tile)
        left = [ref[q, span, :] for ref in (before, after) for q in range(ref.shape[0])]
        total = jnp.dot(jnp.concatenate(left, axis=1), grad_ref[...], preferred_element_type=jnp.float32)
        out_ref[span, :] = total.astype(jnp.bfloat16)
        return carry

    lax.fori_loop(0, NB * BLK // tile, rows, 0)


def grad(before, after, pooled_grad, tile=512):
    return pl.pallas_call(
        functools.partial(grad_body, tile),
        in_specs=[VMEM, VMEM, VMEM],
        out_specs=VMEM,
        out_shape=jax.ShapeDtypeStruct((NB * BLK, E), jnp.bfloat16),
        cost_estimate=pl.CostEstimate(
            flops=2 * pooled_grad.size * NB * BLK, bytes_accessed=pooled_grad.size * 4, transcendentals=0
        ),
        compiler_params=pltpu.CompilerParams(vmem_limit_bytes=8 << 20),
        name="grad",
    )(before, after, pooled_grad)


def pick_body(pair_ref, ids_ref, sect_ref, state_ref, accum_ref, copies_ref, order_ref, out_ref):
    partner = pair_ref[lax.axis_index("table")]
    for n in range(copies_ref.shape[0]):
        copies_ref[n] = sect_ref[partner]
    for j in range(SLAB):
        order_ref[j] = ids_ref[j, partner]
    count = out_ref.shape[0]
    for n in range(count):
        block = lax.axis_index("dp") * count + n
        own = accum_ref[pl.ds(jnp.minimum(block, R - 1), 1), :]
        fold = pl.multiple_of(ids_ref[jnp.maximum(block - R, 0), partner] * BLK, BLK)
        states = state_ref[:, pl.ds(fold, BLK)]
        mine = lax.broadcasted_iota(jnp.int32, states.shape, 0) == partner
        other = jnp.sum(jnp.where(mine, states, 0.0), axis=0, keepdims=True)
        out_ref[n : n + 1, :] = jnp.where(block < R, own, other)


def pick(fold_pairs, slab_ids, sectioned_rows, sectioned_accum, own_accum, parts):
    _, size, width = sectioned_rows.shape
    return pl.pallas_call(
        pick_body,
        in_specs=[SMEM, SMEM, VMEM, VMEM, VMEM],
        out_specs=[VMEM, SMEM, VMEM],
        out_shape=[
            jax.ShapeDtypeStruct((parts, size, width), jnp.bfloat16),
            jax.ShapeDtypeStruct((SLAB,), jnp.int32),
            jax.ShapeDtypeStruct((NB // parts, BLK), jnp.float32),
        ],
        name="pick",
    )(fold_pairs, slab_ids.T, sectioned_rows, sectioned_accum, own_accum.reshape(R, BLK))


def update_body(part_ref, row_ref, accum_ref, new_ref, out_ref):
    for n in range(accum_ref.shape[0]):
        span = slice(n * BLK, (n + 1) * BLK)
        total = part_ref[0, span, :].astype(jnp.float32)
        for q in range(1, part_ref.shape[0]):
            total = total + part_ref[q, span, :].astype(jnp.float32)
        before = jnp.broadcast_to(accum_ref[n : n + 1, :], (BLK, BLK)).T
        accum = before + jnp.mean(total * total, axis=1, keepdims=True)
        out_ref[n : n + 1, :] = accum.T[0:1, :]
        step_size = learn_rate / (jnp.sqrt(accum) + ada_epsilon)
        new_ref[span, :] = (row_ref[span, :].astype(jnp.float32) - step_size * total).astype(jnp.bfloat16)


def update(received, rows, accum):
    return pl.pallas_call(
        update_body,
        in_specs=[VMEM, VMEM, VMEM],
        out_specs=[VMEM, VMEM],
        out_shape=[
            jax.ShapeDtypeStruct(rows.shape, jnp.bfloat16),
            jax.ShapeDtypeStruct(accum.shape, jnp.float32),
        ],
        compiler_params=pltpu.CompilerParams(vmem_limit_bytes=8 << 20),
        name="update",
    )(received, rows, accum)


def lay_body(near_ref, *refs):
    out_ref = refs[-1]
    size = near_ref.shape[0] // 2
    me = lax.axis_index("dp")
    across = out_ref.shape[0] // (2 * size)
    for step, ref in enumerate((near_ref,) + refs[:-1]):
        there = lax.rem(me // 2 + across - step, across) * 2
        for half, side in enumerate((lax.rem(me, 2), 1 - lax.rem(me, 2))):
            at = pl.multiple_of((there + side) * size, size)
            out_ref[pl.ds(at, size), :] = ref[half * size : (half + 1) * size, :]


def spread_rows(rows, parts):
    def along(block, step):
        return lax.ppermute(block, "dp", [(n, (n + 2 * step) % parts) for n in range(parts)])

    other = lax.ppermute(rows, "dp", [(n, n ^ 1) for n in range(parts)])
    near = jnp.concatenate([rows, other], axis=0)
    across = parts // 2
    order = [1, across - 1] + list(range(2, across - 1))
    far = dict((step, along(near, step)) for step in order)
    return pl.pallas_call(
        lay_body,
        in_specs=[VMEM] * across,
        out_specs=VMEM,
        out_shape=jax.ShapeDtypeStruct((parts * rows.shape[0], rows.shape[1]), rows.dtype),
        compiler_params=pltpu.CompilerParams(vmem_limit_bytes=8 << 20),
        name="lay",
    )(near, *[far[step] for step in range(1, across)])


def swap(blocks, axis):
    return lax.all_to_all(blocks, axis, split_axis=0, concat_axis=0, tiled=True)


def shards(
    own_table,
    own_accum,
    sectioned_rows,
    sectioned_accum,
    fold_pairs,
    slab_ids,
    bag_blocks,
    bag_counts,
    bag_weights,
    top_weight,
    hidden_grad,
):
    tables = lax.axis_size("table")
    parts = lax.axis_size("dp")
    share = NB * BLK // parts
    bag_total = bag_blocks.shape[0]
    copies, order, accum = pick(fold_pairs, slab_ids, sectioned_rows, sectioned_accum, own_accum, parts)
    slab_rows = swap(copies, "dp").reshape(SLAB * BLK, E)
    blocks = bag_blocks[:, 0, :].T
    counts = bag_counts.reshape(1, bag_total)
    weights = bag_weights.reshape(bag_total * K, BLK)
    parts_turned = early(weights)
    pooled, before, after, rows = pool(order, blocks, counts, own_table, slab_rows, parts_turned, share)
    fan = swap(pooled.reshape(tables, bag_total // tables, E), "table")
    hidden, back = layer(fan, top_weight, hidden_grad)
    row_grad = grad(before, after, swap(back, "table").reshape(bag_total, E))
    received = swap(row_grad.reshape(parts, share, E), "dp")
    new_rows, accum = update(received, rows, accum)
    new_table = spread_rows(new_rows, parts)
    return (new_table, accum.reshape(share), hidden)


def solution(mesh):
    placed = (
        P("table", None),
        P("table"),
        P(None, "dp", None),
        P(),
        P(),
        P(),
        P("dp", "table", None),
        P("dp", "table"),
        P("dp", "table", None, None),
        P(),
        P(("dp", "table"), None),
    )
    return jax.shard_map(
        shards,
        mesh=mesh,
        in_specs=placed,
        out_specs=(P("table", None), P(("table", "dp")), P(("dp", "table"), None)),
        check_vma=False,
    )
```

```python
import functools

import jax
import jax.numpy as jnp
from jax import lax
from jax.experimental import pallas as pl
from jax.experimental.pallas import tpu as pltpu
from jax.sharding import PartitionSpec as P

E = 128
BLK = 128
R = 10
SLAB = 6
K = 4
NB = R + SLAB
TILE = 16
EACH = 4
FRONT = 8
WIDE = K * BLK

learn_rate = 0.5
ada_epsilon = 1e-08

ANY = pl.BlockSpec(memory_space=pl.ANY)
HBM = pl.BlockSpec(memory_space=pltpu.HBM)
SMEM = pl.BlockSpec(memory_space=pltpu.SMEM)
VMEM = pl.BlockSpec(memory_space=pltpu.VMEM)


def fill_perm(perm_ref):
    row = lax.broadcasted_iota(jnp.int32, (WIDE, BLK), 0)
    lane = lax.broadcasted_iota(jnp.int32, (WIDE, BLK), 1)
    for k in range(K):
        perm_ref[k] = jnp.where(row == lane * K + k, 1.0, 0.0).astype(jnp.bfloat16)


def turn(window, at, perm_ref, part_ref, group):
    turned = jnp.concatenate([window[pl.ds(at + BLK * n, BLK), :].T for n in range(K)], axis=1)
    for k in range(0, K, 2):
        right = jnp.concatenate([perm_ref[k], perm_ref[k + 1]], axis=1)
        got = jnp.dot(turned, right, preferred_element_type=jnp.float32).astype(jnp.bfloat16)
        part_ref[group, k] = got[:, :BLK]
        part_ref[group, k + 1] = got[:, BLK:]


def place(block_ref, count_ref, base, part_ref, group, out_ref, at):
    blocks = block_ref[:, pl.ds(base, BLK)]
    counts = count_ref[:, pl.ds(base, BLK)]
    names = []
    for k in range(K):
        name = jnp.where(counts > k, blocks[k : k + 1, :], NB).astype(jnp.float32)
        names.append(jnp.broadcast_to(name, (TILE, BLK)).astype(jnp.bfloat16))
    for m in range(NB):
        hits = [names[k] == jnp.bfloat16(m) for k in range(K)]
        for s in range(0, BLK, TILE):
            value = jnp.zeros((TILE, BLK), jnp.bfloat16)
            for k in range(K):
                value = jnp.where(hits[k], part_ref[group, k, s : s + TILE, :], value)
            out_ref[at, m * BLK + s : m * BLK + s + TILE, :] = value


def fetches(source, base, target, sem, pieces):
    size = target.shape[0] // pieces

    def piece(n):
        return pltpu.make_async_copy(
            source.at[pl.ds(base + n * size, size)], target.at[pl.ds(n * size, size)], sem.at[n]
        )

    return piece


def early_body(block_ref, count_ref, weight_hbm, front_hbm, out_hbm, window, perm_ref, near_ref, front, part_ref, in_sem, front_sem, out_sem):
    ahead = front.shape[0] // EACH
    rest = part_ref.shape[0] // EACH
    fetch = fetches(weight_hbm, 0, window, in_sem, ahead + rest)

    def send(source, target, sem, piece):
        span = pl.ds(pl.multiple_of(piece * EACH, EACH), EACH)
        return pltpu.make_async_copy(source.at[span], target.at[span], sem.at[piece])

    for n in range(ahead + rest):
        fetch(n).start()
    fill_perm(perm_ref)

    def lead(piece, carry):
        fetch(piece).wait()
        for g in range(EACH):
            turn(window, pl.multiple_of((piece * EACH + g) * WIDE, WIDE), perm_ref, near_ref, g)
        for g in range(EACH):
            group = piece * EACH + g
            place(block_ref, count_ref, pl.multiple_of(group * BLK, BLK), near_ref, g, front, group)
        send(front, front_hbm, front_sem, piece).start()
        return carry

    lax.fori_loop(0, ahead, lead, 0)

    def step(piece, carry):
        fetch(ahead + piece).wait()
        for g in range(EACH):
            group = piece * EACH + g
            at = pl.multiple_of((ahead * EACH + group) * WIDE, WIDE)
            turn(window, at, perm_ref, part_ref, group)
        send(part_ref, out_hbm, out_sem, piece).start()
        return carry

    lax.fori_loop(0, rest, step, 0)
    for n in range(ahead):
        send(front, front_hbm, front_sem, n).wait()
    for n in range(rest):
        send(part_ref, out_hbm, out_sem, n).wait()


def early(blocks, counts, weights):
    groups = weights.shape[0] // WIDE
    parts = (groups - FRONT, K, BLK, BLK)
    front = (FRONT, NB * BLK, BLK)
    return pl.pallas_call(
        early_body,
        in_specs=[VMEM, VMEM, HBM],
        out_specs=[HBM, HBM],
        out_shape=[jax.ShapeDtypeStruct(front, jnp.bfloat16), jax.ShapeDtypeStruct(parts, jnp.bfloat16)],
        scratch_shapes=[
            pltpu.VMEM(weights.shape, jnp.bfloat16),
            pltpu.VMEM((K, WIDE, BLK), jnp.bfloat16),
            pltpu.VMEM((EACH, K, BLK, BLK), jnp.bfloat16),
            pltpu.VMEM(front, jnp.bfloat16),
            pltpu.VMEM(parts, jnp.bfloat16),
            pltpu.SemaphoreType.DMA((groups // EACH,)),
            pltpu.SemaphoreType.DMA((FRONT // EACH,)),
            pltpu.SemaphoreType.DMA((parts[0] // EACH,)),
        ],
        cost_estimate=pl.CostEstimate(
            flops=2 * weights.size * WIDE * 4, bytes_accessed=weights.size * 4, transcendentals=0
        ),
        name="early",
    )(blocks, counts, weights)


def pool_body(
    order_ref, block_ref, count_ref, own_ref, slab_ref, front_hbm, part_hbm,
    pooled, first, second, share_ref,
    part_ref, table_ref, turned_ref, front_sem, part_sem,
):
    half = first.shape[0]
    pieces = (2 * half - FRONT) // EACH
    fetch = fetches(part_hbm, 0, part_ref, part_sem, pieces)
    again = fetches(front_hbm, 0, first.at[pl.ds(0, FRONT)], front_sem, FRONT // 2)
    lead = (half - FRONT) // EACH
    for n in range(lead):
        fetch(n).start()
    for n in range(FRONT // 2):
        again(n).start()
    for n in range(lead, pieces):
        fetch(n).start()
    table_ref[0 : R * BLK, :] = own_ref[...]
    for j in range(SLAB):
        at = pl.multiple_of(order_ref[j] * BLK, BLK)
        table_ref[(R + j) * BLK : (R + j + 1) * BLK, :] = slab_ref[pl.ds(at, BLK), :]
    for m in range(NB):
        turned_ref[:, m * BLK : (m + 1) * BLK] = table_ref[m * BLK : (m + 1) * BLK, :].T
    share = share_ref.shape[0]
    share_ref[...] = table_ref[pl.ds(pl.multiple_of(lax.axis_index("dp") * share, share), share), :]

    def sums(source, at, count, to):
        right = jnp.concatenate([source[at + q] for q in range(count)], axis=1)
        got = jnp.dot(turned_ref[...], right, preferred_element_type=jnp.float32)
        pooled[pl.ds(pl.multiple_of(to * BLK, BLK), count * BLK), :] = got.T.astype(jnp.bfloat16)

    def put(group, target, at):
        place(block_ref, count_ref, pl.multiple_of(group * BLK, BLK), part_ref, group - FRONT, target, at)

    def fill(pair, carry):
        @pl.when(lax.rem(pair, EACH // 2) == 0)
        def _():
            fetch(pair // (EACH // 2) - FRONT // EACH).wait()

        for g in range(2):
            put(2 * pair + g, first, 2 * pair + g)
        return carry

    lax.fori_loop(FRONT // 2, half // 2, fill, 0)
    for n in range(FRONT // 2):
        again(n).wait()

    def both(pair, carry):
        @pl.when(lax.rem(pair, EACH // 2) == 0)
        def _():
            fetch(lead + pair // (EACH // 2)).wait()

        for g in range(2):
            put(half + 2 * pair + g, second, 2 * pair + g)
        sums(first, 2 * pair, 2, 2 * pair)
        return carry

    lax.fori_loop(0, half // 2, both, 0)

    def rest(n, carry):
        sums(second, 4 * n, 4, half + 4 * n)
        return carry

    lax.fori_loop(0, half // 4, rest, 0)


def pool(order, blocks, counts, own, slab, front, parts, share):
    bags = blocks.shape[1]
    matrix = pltpu.VMEM((bags // (2 * BLK), NB * BLK, BLK), jnp.bfloat16)
    return pl.pallas_call(
        pool_body,
        in_specs=[SMEM, VMEM, VMEM, VMEM, VMEM, HBM, HBM],
        out_specs=[VMEM, VMEM, VMEM, VMEM],
        out_shape=[
            jax.ShapeDtypeStruct((bags, E), jnp.bfloat16),
            matrix,
            matrix,
            jax.ShapeDtypeStruct((share, E), jnp.bfloat16),
        ],
        scratch_shapes=[
            pltpu.VMEM(parts.shape, jnp.bfloat16),
            pltpu.VMEM((NB * BLK, E), jnp.bfloat16),
            pltpu.VMEM((E, NB * BLK), jnp.bfloat16),
            pltpu.SemaphoreType.DMA((FRONT // 2,)),
            pltpu.SemaphoreType.DMA((parts.shape[0] // EACH,)),
        ],
        cost_estimate=pl.CostEstimate(
            flops=2 * bags * NB * BLK * E, bytes_accessed=bags * NB * BLK * 2, transcendentals=0
        ),
        compiler_params=pltpu.CompilerParams(vmem_limit_bytes=36 << 20),
        name="pool",
    )(order, blocks, counts, own, slab, front, parts)


def layer_body(pair, fan_ref, top_ref, cot_ref, hid_hbm, out_ref, hid_ref, sum_ref, pre_ref, sem):
    fan, rows, _ = fan_ref.shape
    wide = pair * E
    steps = fan // pair
    send_hid = pltpu.make_async_copy(hid_ref, hid_hbm, sem)
    for p in range(steps):
        left = jnp.concatenate([fan_ref[p * pair + q] for q in range(pair)], axis=1)
        part = jnp.dot(left, top_ref[p * wide : (p + 1) * wide, :], preferred_element_type=jnp.float32)
        if p == 0:
            sum_ref[...] = part
        else:
            sum_ref[...] += part
    preact = sum_ref[...]
    gate = jax.nn.sigmoid(preact)
    hid_ref[...] = (preact * gate).astype(jnp.bfloat16)
    send_hid.start()
    slope = gate * (1.0 + preact * (1.0 - gate))
    pre_ref[...] = (cot_ref[...].astype(jnp.float32) * slope).astype(jnp.bfloat16)
    for p in range(steps):
        back = lax.dot_general(
            pre_ref[...],
            top_ref[p * wide : (p + 1) * wide, :],
            (((1,), (1,)), ((), ())),
            preferred_element_type=jnp.float32,
        ).astype(jnp.bfloat16)
        for q in range(pair):
            out_ref[p * pair + q] = back[:, q * E : (q + 1) * E]
    send_hid.wait()


def layer(fan, top_weight, cotangent, pair=4):
    tables, rows, _ = fan.shape
    hidden = top_weight.shape[1]
    return pl.pallas_call(
        functools.partial(layer_body, pair),
        in_specs=[VMEM, VMEM, VMEM],
        out_specs=[HBM, VMEM],
        out_shape=[
            jax.ShapeDtypeStruct((rows, hidden), jnp.bfloat16),
            jax.ShapeDtypeStruct((tables, rows, E), jnp.bfloat16),
        ],
        scratch_shapes=[
            pltpu.VMEM((rows, hidden), jnp.bfloat16),
            pltpu.VMEM((rows, hidden), jnp.float32),
            pltpu.VMEM((rows, hidden), jnp.bfloat16),
            pltpu.SemaphoreType.DMA,
        ],
        cost_estimate=pl.CostEstimate(
            flops=4 * rows * top_weight.size, bytes_accessed=rows * hidden * 6, transcendentals=rows * hidden
        ),
        compiler_params=pltpu.CompilerParams(vmem_limit_bytes=16 << 20),
        name="layer",
    )(fan, top_weight, cotangent)


def grad_body(tile, before, after, grad_ref, out_ref):
    def rows(n, carry):
        span = pl.ds(pl.multiple_of(n * tile, tile), tile)
        left = [ref[q, span, :] for ref in (before, after) for q in range(ref.shape[0])]
        total = jnp.dot(jnp.concatenate(left, axis=1), grad_ref[...], preferred_element_type=jnp.float32)
        out_ref[span, :] = total.astype(jnp.bfloat16)
        return carry

    lax.fori_loop(0, NB * BLK // tile, rows, 0)


def grad(before, after, pooled_grad, tile=512):
    return pl.pallas_call(
        functools.partial(grad_body, tile),
        in_specs=[VMEM, VMEM, VMEM],
        out_specs=VMEM,
        out_shape=jax.ShapeDtypeStruct((NB * BLK, E), jnp.bfloat16),
        cost_estimate=pl.CostEstimate(
            flops=2 * pooled_grad.size * NB * BLK, bytes_accessed=pooled_grad.size * 4, transcendentals=0
        ),
        compiler_params=pltpu.CompilerParams(vmem_limit_bytes=8 << 20),
        name="grad",
    )(before, after, pooled_grad)


def pick_body(pair_ref, ids_ref, sect_ref, state_ref, accum_ref, copies_ref, order_ref, out_ref):
    partner = pair_ref[lax.axis_index("table")]
    for n in range(copies_ref.shape[0]):
        copies_ref[n] = sect_ref[partner]
    for j in range(SLAB):
        order_ref[j] = ids_ref[j, partner]
    count = out_ref.shape[0]
    for n in range(count):
        block = lax.axis_index("dp") * count + n
        own = accum_ref[pl.ds(jnp.minimum(block, R - 1), 1), :]
        fold = pl.multiple_of(ids_ref[jnp.maximum(block - R, 0), partner] * BLK, BLK)
        states = state_ref[:, pl.ds(fold, BLK)]
        mine = lax.broadcasted_iota(jnp.int32, states.shape, 0) == partner
        other = jnp.sum(jnp.where(mine, states, 0.0), axis=0, keepdims=True)
        out_ref[n : n + 1, :] = jnp.where(block < R, own, other)


def pick(fold_pairs, slab_ids, sectioned_rows, sectioned_accum, own_accum, parts):
    _, size, width = sectioned_rows.shape
    return pl.pallas_call(
        pick_body,
        in_specs=[SMEM, SMEM, VMEM, VMEM, VMEM],
        out_specs=[VMEM, SMEM, VMEM],
        out_shape=[
            jax.ShapeDtypeStruct((parts, size, width), jnp.bfloat16),
            jax.ShapeDtypeStruct((SLAB,), jnp.int32),
            jax.ShapeDtypeStruct((NB // parts, BLK), jnp.float32),
        ],
        name="pick",
    )(fold_pairs, slab_ids.T, sectioned_rows, sectioned_accum, own_accum.reshape(R, BLK))


def update_body(part_ref, row_ref, accum_ref, new_ref, out_ref):
    for n in range(accum_ref.shape[0]):
        span = slice(n * BLK, (n + 1) * BLK)
        total = part_ref[0, span, :].astype(jnp.float32)
        for q in range(1, part_ref.shape[0]):
            total = total + part_ref[q, span, :].astype(jnp.float32)
        before = jnp.broadcast_to(accum_ref[n : n + 1, :], (BLK, BLK)).T
        accum = before + jnp.mean(total * total, axis=1, keepdims=True)
        out_ref[n : n + 1, :] = accum.T[0:1, :]
        step_size = learn_rate / (jnp.sqrt(accum) + ada_epsilon)
        new_ref[span, :] = (row_ref[span, :].astype(jnp.float32) - step_size * total).astype(jnp.bfloat16)


def update(received, rows, accum):
    return pl.pallas_call(
        update_body,
        in_specs=[VMEM, VMEM, VMEM],
        out_specs=[VMEM, VMEM],
        out_shape=[
            jax.ShapeDtypeStruct(rows.shape, jnp.bfloat16),
            jax.ShapeDtypeStruct(accum.shape, jnp.float32),
        ],
        compiler_params=pltpu.CompilerParams(vmem_limit_bytes=8 << 20),
        name="update",
    )(received, rows, accum)


def lay_body(near_ref, *refs):
    refs, (out_hbm, sem) = refs[:-2], refs[-2:]
    size = near_ref.shape[0] // 2
    me = lax.axis_index("dp")
    across = out_hbm.shape[0] // (2 * size)
    copies = []
    for step, ref in enumerate((near_ref,) + tuple(refs)):
        there = lax.rem(me // 2 + across - step, across) * 2
        for half, side in enumerate((lax.rem(me, 2), 1 - lax.rem(me, 2))):
            at = pl.multiple_of((there + side) * size, size)
            source = ref.at[pl.ds(half * size, size), :]
            copies.append(pltpu.make_async_copy(source, out_hbm.at[pl.ds(at, size), :], sem.at[step * 2 + half]))
            copies[-1].start()
    for copy in copies:
        copy.wait()


def spread_rows(rows, parts):
    def along(block, step):
        return lax.ppermute(block, "dp", [(n, (n + 2 * step) % parts) for n in range(parts)])

    other = lax.ppermute(rows, "dp", [(n, n ^ 1) for n in range(parts)])
    near = jnp.concatenate([rows, other], axis=0)
    across = parts // 2
    order = [1, across - 1] + list(range(2, across - 1))
    far = dict((step, along(near, step)) for step in order)
    return pl.pallas_call(
        lay_body,
        in_specs=[VMEM] * across,
        out_specs=HBM,
        scratch_shapes=[pltpu.SemaphoreType.DMA((parts,))],
        out_shape=jax.ShapeDtypeStruct((parts * rows.shape[0], rows.shape[1]), rows.dtype),
        compiler_params=pltpu.CompilerParams(vmem_limit_bytes=8 << 20),
        name="lay",
    )(near, *[far[step] for step in range(1, across)])


def swap(blocks, axis):
    return lax.all_to_all(blocks, axis, split_axis=0, concat_axis=0, tiled=True)


def shards(
    own_table,
    own_accum,
    sectioned_rows,
    sectioned_accum,
    fold_pairs,
    slab_ids,
    bag_blocks,
    bag_counts,
    bag_weights,
    top_weight,
    hidden_grad,
):
    tables = lax.axis_size("table")
    parts = lax.axis_size("dp")
    share = NB * BLK // parts
    bag_total = bag_blocks.shape[0]
    copies, order, accum = pick(fold_pairs, slab_ids, sectioned_rows, sectioned_accum, own_accum, parts)
    slab_rows = swap(copies, "dp").reshape(SLAB * BLK, E)
    blocks = bag_blocks[:, 0, :].T
    counts = bag_counts.reshape(1, bag_total)
    weights = bag_weights.reshape(bag_total * K, BLK)
    front, turned = early(blocks, counts, weights)
    pooled, before, after, rows = pool(order, blocks, counts, own_table, slab_rows, front, turned, share)
    fan = swap(pooled.reshape(tables, bag_total // tables, E), "table")
    hidden, back = layer(fan, top_weight, hidden_grad)
    row_grad = grad(before, after, swap(back, "table").reshape(bag_total, E))
    received = swap(row_grad.reshape(parts, share, E), "dp")
    new_rows, accum = update(received, rows, accum)
    new_table = spread_rows(new_rows, parts)
    return (new_table, accum.reshape(share), hidden)


def solution(mesh):
    placed = (
        P("table", None),
        P("table"),
        P(None, "dp", None),
        P(),
        P(),
        P(),
        P("dp", "table", None),
        P("dp", "table"),
        P("dp", "table", None, None),
        P(),
        P(("dp", "table"), None),
    )
    return jax.shard_map(
        shards,
        mesh=mesh,
        in_specs=placed,
        out_specs=(P("table", None), P(("table", "dp")), P(("dp", "table"), None)),
        check_vma=False,
    )
```

```python
import functools

import jax
import jax.numpy as jnp
from jax import lax
from jax.experimental import pallas as pl
from jax.experimental.pallas import tpu as pltpu
from jax.sharding import PartitionSpec as P

E = 128
BLK = 128
R = 10
SLAB = 6
K = 4
NB = R + SLAB
TILE = 16
EACH = 4
WIDE = K * BLK

learn_rate = 0.5
ada_epsilon = 1e-08

ANY = pl.BlockSpec(memory_space=pl.ANY)
HBM = pl.BlockSpec(memory_space=pltpu.HBM)
SMEM = pl.BlockSpec(memory_space=pltpu.SMEM)
VMEM = pl.BlockSpec(memory_space=pltpu.VMEM)


def fill_perm(perm_ref):
    row = lax.broadcasted_iota(jnp.int32, (WIDE, BLK), 0)
    lane = lax.broadcasted_iota(jnp.int32, (WIDE, BLK), 1)
    for k in range(K):
        perm_ref[k] = jnp.where(row == lane * K + k, 1.0, 0.0).astype(jnp.bfloat16)


def turn(window, at, perm_ref, part_ref, group):
    turned = jnp.concatenate([window[pl.ds(at + BLK * n, BLK), :].T for n in range(K)], axis=1)
    for k in range(0, K, 2):
        right = jnp.concatenate([perm_ref[k], perm_ref[k + 1]], axis=1)
        got = jnp.dot(turned, right, preferred_element_type=jnp.float32).astype(jnp.bfloat16)
        part_ref[group, k] = got[:, :BLK]
        part_ref[group, k + 1] = got[:, BLK:]


def place(block_ref, count_ref, base, part_ref, group, out_ref, at):
    blocks = block_ref[:, pl.ds(base, BLK)]
    counts = count_ref[:, pl.ds(base, BLK)]
    names = []
    for k in range(K):
        name = jnp.where(counts > k, blocks[k : k + 1, :], NB).astype(jnp.float32)
        names.append(jnp.broadcast_to(name, (TILE, BLK)).astype(jnp.bfloat16))
    for m in range(NB):
        hits = [names[k] == jnp.bfloat16(m) for k in range(K)]
        for s in range(0, BLK, TILE):
            value = jnp.zeros((TILE, BLK), jnp.bfloat16)
            for k in range(K):
                value = jnp.where(hits[k], part_ref[group, k, s : s + TILE, :], value)
            out_ref[at, m * BLK + s : m * BLK + s + TILE, :] = value


def fetches(source, base, target, sem, pieces):
    size = target.shape[0] // pieces

    def piece(n):
        return pltpu.make_async_copy(
            source.at[pl.ds(base + n * size, size)], target.at[pl.ds(n * size, size)], sem.at[n]
        )

    return piece


def early_body(weight_hbm, out_hbm, window, perm_ref, part_ref, in_sem, out_sem):
    groups = part_ref.shape[0]
    pieces = groups // EACH
    fetch = fetches(weight_hbm, 0, window, in_sem, pieces)

    def send(piece):
        span = pl.ds(pl.multiple_of(piece * EACH, EACH), EACH)
        return pltpu.make_async_copy(part_ref.at[span], out_hbm.at[span], out_sem.at[piece])

    for n in range(pieces):
        fetch(n).start()
    fill_perm(perm_ref)

    def step(piece, carry):
        fetch(piece).wait()
        for g in range(EACH):
            group = piece * EACH + g
            turn(window, pl.multiple_of(group * WIDE, WIDE), perm_ref, part_ref, group)
        send(piece).start()
        return carry

    lax.fori_loop(0, pieces, step, 0)
    for n in range(pieces):
        send(n).wait()


def early(weights):
    groups = weights.shape[0] // WIDE
    parts = (groups, K, BLK, BLK)
    sem = pltpu.SemaphoreType.DMA((groups // EACH,))
    return pl.pallas_call(
        early_body,
        in_specs=[HBM],
        out_specs=ANY,
        out_shape=jax.ShapeDtypeStruct(parts, jnp.bfloat16),
        scratch_shapes=[
            pltpu.VMEM(weights.shape, jnp.bfloat16),
            pltpu.VMEM((K, WIDE, BLK), jnp.bfloat16),
            pltpu.VMEM(parts, jnp.bfloat16),
            sem,
            sem,
        ],
        cost_estimate=pl.CostEstimate(
            flops=2 * weights.size * WIDE * 4, bytes_accessed=weights.size * 4, transcendentals=0
        ),
        name="early",
    )(weights)


def pool_body(
    order_ref, block_ref, count_ref, own_ref, slab_ref, part_hbm,
    pooled, first, second, share_ref,
    part_ref, table_ref, turned_ref, part_sem,
):
    half = first.shape[0]
    pieces = 2 * half // EACH
    fetch = fetches(part_hbm, 0, part_ref, part_sem, pieces)
    for n in range(pieces):
        fetch(n).start()
    table_ref[0 : R * BLK, :] = own_ref[...]
    for j in range(SLAB):
        at = pl.multiple_of(order_ref[j] * BLK, BLK)
        table_ref[(R + j) * BLK : (R + j + 1) * BLK, :] = slab_ref[pl.ds(at, BLK), :]
    for m in range(NB):
        turned_ref[:, m * BLK : (m + 1) * BLK] = table_ref[m * BLK : (m + 1) * BLK, :].T
    share = share_ref.shape[0]
    share_ref[...] = table_ref[pl.ds(pl.multiple_of(lax.axis_index("dp") * share, share), share), :]

    def sums(source, at, count, to):
        right = jnp.concatenate([source[at + q] for q in range(count)], axis=1)
        got = jnp.dot(turned_ref[...], right, preferred_element_type=jnp.float32)
        pooled[pl.ds(pl.multiple_of(to * BLK, BLK), count * BLK), :] = got.T.astype(jnp.bfloat16)

    def put(group, target, at):
        place(block_ref, count_ref, pl.multiple_of(group * BLK, BLK), part_ref, group, target, at)

    def fill(pair, carry):
        @pl.when(lax.rem(pair, EACH // 2) == 0)
        def _():
            fetch(pair // (EACH // 2)).wait()

        for g in range(2):
            put(2 * pair + g, first, 2 * pair + g)
        return carry

    lax.fori_loop(0, half // 2, fill, 0)

    def both(pair, carry):
        @pl.when(lax.rem(pair, EACH // 2) == 0)
        def _():
            fetch(half // EACH + pair // (EACH // 2)).wait()

        for g in range(2):
            put(half + 2 * pair + g, second, 2 * pair + g)
        sums(first, 2 * pair, 2, 2 * pair)
        return carry

    lax.fori_loop(0, half // 2, both, 0)

    def rest(n, carry):
        sums(second, 4 * n, 4, half + 4 * n)
        return carry

    lax.fori_loop(0, half // 4, rest, 0)


def pool(order, blocks, counts, own, slab, parts, share):
    bags = blocks.shape[1]
    matrix = pltpu.VMEM((bags // (2 * BLK), NB * BLK, BLK), jnp.bfloat16)
    return pl.pallas_call(
        pool_body,
        in_specs=[SMEM, VMEM, VMEM, VMEM, VMEM, HBM],
        out_specs=[VMEM, VMEM, VMEM, VMEM],
        out_shape=[
            jax.ShapeDtypeStruct((bags, E), jnp.bfloat16),
            matrix,
            matrix,
            jax.ShapeDtypeStruct((share, E), jnp.bfloat16),
        ],
        scratch_shapes=[
            pltpu.VMEM(parts.shape, jnp.bfloat16),
            pltpu.VMEM((NB * BLK, E), jnp.bfloat16),
            pltpu.VMEM((E, NB * BLK), jnp.bfloat16),
            pltpu.SemaphoreType.DMA((parts.shape[0] // EACH,)),
        ],
        cost_estimate=pl.CostEstimate(
            flops=2 * bags * NB * BLK * E, bytes_accessed=bags * NB * BLK * 2, transcendentals=0
        ),
        compiler_params=pltpu.CompilerParams(vmem_limit_bytes=36 << 20),
        name="pool",
    )(order, blocks, counts, own, slab, parts)


def layer_body(pair, fan_ref, top_ref, cot_ref, hid_hbm, out_ref, hid_ref, sum_ref, pre_ref, sem):
    fan, rows, _ = fan_ref.shape
    wide = pair * E
    steps = fan // pair
    send_hid = pltpu.make_async_copy(hid_ref, hid_hbm, sem)
    for p in range(steps):
        left = jnp.concatenate([fan_ref[p * pair + q] for q in range(pair)], axis=1)
        part = jnp.dot(left, top_ref[p * wide : (p + 1) * wide, :], preferred_element_type=jnp.float32)
        if p == 0:
            sum_ref[...] = part
        else:
            sum_ref[...] += part
    preact = sum_ref[...]
    gate = jax.nn.sigmoid(preact)
    hid_ref[...] = (preact * gate).astype(jnp.bfloat16)
    send_hid.start()
    slope = gate * (1.0 + preact * (1.0 - gate))
    pre_ref[...] = (cot_ref[...].astype(jnp.float32) * slope).astype(jnp.bfloat16)
    for p in range(steps):
        back = lax.dot_general(
            pre_ref[...],
            top_ref[p * wide : (p + 1) * wide, :],
            (((1,), (1,)), ((), ())),
            preferred_element_type=jnp.float32,
        ).astype(jnp.bfloat16)
        for q in range(pair):
            out_ref[p * pair + q] = back[:, q * E : (q + 1) * E]
    send_hid.wait()


def layer(fan, top_weight, cotangent, pair=4):
    tables, rows, _ = fan.shape
    hidden = top_weight.shape[1]
    return pl.pallas_call(
        functools.partial(layer_body, pair),
        in_specs=[VMEM, VMEM, VMEM],
        out_specs=[HBM, VMEM],
        out_shape=[
            jax.ShapeDtypeStruct((rows, hidden), jnp.bfloat16),
            jax.ShapeDtypeStruct((tables, rows, E), jnp.bfloat16),
        ],
        scratch_shapes=[
            pltpu.VMEM((rows, hidden), jnp.bfloat16),
            pltpu.VMEM((rows, hidden), jnp.float32),
            pltpu.VMEM((rows, hidden), jnp.bfloat16),
            pltpu.SemaphoreType.DMA,
        ],
        cost_estimate=pl.CostEstimate(
            flops=4 * rows * top_weight.size, bytes_accessed=rows * hidden * 6, transcendentals=rows * hidden
        ),
        compiler_params=pltpu.CompilerParams(vmem_limit_bytes=16 << 20),
        name="layer",
    )(fan, top_weight, cotangent)


def grad_body(tile, before, after, grad_ref, out_ref):
    def rows(n, carry):
        span = pl.ds(pl.multiple_of(n * tile, tile), tile)
        left = [ref[q, span, :] for ref in (before, after) for q in range(ref.shape[0])]
        total = jnp.dot(jnp.concatenate(left, axis=1), grad_ref[...], preferred_element_type=jnp.float32)
        out_ref[span, :] = total.astype(jnp.bfloat16)
        return carry

    lax.fori_loop(0, NB * BLK // tile, rows, 0)


def grad(before, after, pooled_grad, tile=512):
    return pl.pallas_call(
        functools.partial(grad_body, tile),
        in_specs=[VMEM, VMEM, VMEM],
        out_specs=VMEM,
        out_shape=jax.ShapeDtypeStruct((NB * BLK, E), jnp.bfloat16),
        cost_estimate=pl.CostEstimate(
            flops=2 * pooled_grad.size * NB * BLK, bytes_accessed=pooled_grad.size * 4, transcendentals=0
        ),
        compiler_params=pltpu.CompilerParams(vmem_limit_bytes=8 << 20),
        name="grad",
    )(before, after, pooled_grad)


def pick_body(pair_ref, ids_ref, sect_ref, state_ref, accum_ref, piece_ref, order_ref, out_ref):
    partner = pair_ref[lax.axis_index("table")]
    piece_ref[...] = sect_ref[partner]
    for j in range(SLAB):
        order_ref[j] = ids_ref[j, partner]
    count = out_ref.shape[0]
    for n in range(count):
        block = lax.axis_index("dp") * count + n
        own = accum_ref[pl.ds(jnp.minimum(block, R - 1), 1), :]
        fold = pl.multiple_of(ids_ref[jnp.maximum(block - R, 0), partner] * BLK, BLK)
        states = state_ref[:, pl.ds(fold, BLK)]
        mine = lax.broadcasted_iota(jnp.int32, states.shape, 0) == partner
        other = jnp.sum(jnp.where(mine, states, 0.0), axis=0, keepdims=True)
        out_ref[n : n + 1, :] = jnp.where(block < R, own, other)


def pick(fold_pairs, slab_ids, sectioned_rows, sectioned_accum, own_accum, parts):
    _, size, width = sectioned_rows.shape
    return pl.pallas_call(
        pick_body,
        in_specs=[SMEM, SMEM, VMEM, VMEM, VMEM],
        out_specs=[VMEM, SMEM, VMEM],
        out_shape=[
            jax.ShapeDtypeStruct((size, width), jnp.bfloat16),
            jax.ShapeDtypeStruct((SLAB,), jnp.int32),
            jax.ShapeDtypeStruct((NB // parts, BLK), jnp.float32),
        ],
        name="pick",
    )(fold_pairs, slab_ids.T, sectioned_rows, sectioned_accum, own_accum.reshape(R, BLK))


def update_body(part_ref, row_ref, accum_ref, new_ref, out_ref):
    for n in range(accum_ref.shape[0]):
        span = slice(n * BLK, (n + 1) * BLK)
        total = part_ref[0, span, :].astype(jnp.float32)
        for q in range(1, part_ref.shape[0]):
            total = total + part_ref[q, span, :].astype(jnp.float32)
        before = jnp.broadcast_to(accum_ref[n : n + 1, :], (BLK, BLK)).T
        accum = before + jnp.mean(total * total, axis=1, keepdims=True)
        out_ref[n : n + 1, :] = accum.T[0:1, :]
        step_size = learn_rate / (jnp.sqrt(accum) + ada_epsilon)
        new_ref[span, :] = (row_ref[span, :].astype(jnp.float32) - step_size * total).astype(jnp.bfloat16)


def update(received, rows, accum):
    return pl.pallas_call(
        update_body,
        in_specs=[VMEM, VMEM, VMEM],
        out_specs=[VMEM, VMEM],
        out_shape=[
            jax.ShapeDtypeStruct(rows.shape, jnp.bfloat16),
            jax.ShapeDtypeStruct(accum.shape, jnp.float32),
        ],
        compiler_params=pltpu.CompilerParams(vmem_limit_bytes=8 << 20),
        name="update",
    )(received, rows, accum)


def lay_body(near_ref, *refs):
    out_ref = refs[-1]
    size = near_ref.shape[0] // 2
    me = lax.axis_index("dp")
    across = out_ref.shape[0] // (2 * size)
    for step, ref in enumerate((near_ref,) + refs[:-1]):
        there = lax.rem(me // 2 + across - step, across) * 2
        for half, side in enumerate((lax.rem(me, 2), 1 - lax.rem(me, 2))):
            at = pl.multiple_of((there + side) * size, size)
            out_ref[pl.ds(at, size), :] = ref[half * size : (half + 1) * size, :]


def spread_rows(rows, parts, beside=()):
    def along(block, step):
        return lax.ppermute(block, "dp", [(n, (n + 2 * step) % parts) for n in range(parts)])

    other = lax.ppermute(rows, "dp", [(n, n ^ 1) for n in range(parts)])
    near = jnp.concatenate([rows, other], axis=0)
    if beside:
        near, *beside = lax.optimization_barrier((near, *beside))
    across = parts // 2
    order = [1, across - 1] + list(range(2, across - 1))
    far = dict((step, along(near, step)) for step in order)
    laid = pl.pallas_call(
        lay_body,
        in_specs=[VMEM] * across,
        out_specs=VMEM,
        out_shape=jax.ShapeDtypeStruct((parts * rows.shape[0], rows.shape[1]), rows.dtype),
        compiler_params=pltpu.CompilerParams(vmem_limit_bytes=8 << 20),
        name="lay",
    )(near, *[far[step] for step in range(1, across)])
    return laid, beside


def swap(blocks, axis):
    return lax.all_to_all(blocks, axis, split_axis=0, concat_axis=0, tiled=True)


def shards(
    own_table,
    own_accum,
    sectioned_rows,
    sectioned_accum,
    fold_pairs,
    slab_ids,
    bag_blocks,
    bag_counts,
    bag_weights,
    top_weight,
    hidden_grad,
):
    tables = lax.axis_size("table")
    parts = lax.axis_size("dp")
    share = NB * BLK // parts
    bag_total = bag_blocks.shape[0]
    piece, order, accum = pick(fold_pairs, slab_ids, sectioned_rows, sectioned_accum, own_accum, parts)
    blocks = bag_blocks[:, 0, :].T
    counts = bag_counts.reshape(1, bag_total)
    weights = bag_weights.reshape(bag_total * K, BLK)
    slab_rows, (weights,) = spread_rows(piece, parts, (weights,))
    parts_turned = early(weights)
    pooled, before, after, rows = pool(order, blocks, counts, own_table, slab_rows, parts_turned, share)
    fan = swap(pooled.reshape(tables, bag_total // tables, E), "table")
    hidden, back = layer(fan, top_weight, hidden_grad)
    row_grad = grad(before, after, swap(back, "table").reshape(bag_total, E))
    received = swap(row_grad.reshape(parts, share, E), "dp")
    new_rows, accum = update(received, rows, accum)
    new_table, _ = spread_rows(new_rows, parts)
    return (new_table, accum.reshape(share), hidden)


def solution(mesh):
    placed = (
        P("table", None),
        P("table"),
        P(None, "dp", None),
        P(),
        P(),
        P(),
        P("dp", "table", None),
        P("dp", "table"),
        P("dp", "table", None, None),
        P(),
        P(("dp", "table"), None),
    )
    return jax.shard_map(
        shards,
        mesh=mesh,
        in_specs=placed,
        out_specs=(P("table", None), P(("table", "dp")), P(("dp", "table"), None)),
        check_vma=False,
    )
```
